32 devices in a mesh: dp: 8 (over y, x, core), seq: 4 (over z).
Axes of the slice: x: 2, y: 2, z: 4, core: 2. Of those that a mesh axis runs over, the one named last changes fastest.
Arguments:
- tokens: bfloat16 [8, 2048, 1024], P('dp', 'seq'), may hold values from -45 to 45
- expand_value: bfloat16 [1024, 2816], P(None, 'dp'), may hold values from -0.1875 to 0.1875
- expand_scale: bfloat16 [8, 2816], P(None, 'dp'), may hold values from 0.5 to 2
- shrink_value: bfloat16 [2816, 1024], P(None, 'dp'), may hold values from -0.109375 to 0.109375
- shrink_scale: bfloat16 [22, 1024], P(None, 'dp'), may hold values from 0.5 to 2
- project_value: bfloat16 [1024, 3072], P(None, 'dp'), may hold values from -0.1875 to 0.1875
- project_scale: bfloat16 [8, 3072], P(None, 'dp'), may hold values from 0.5 to 12, as said below
- output_value: bfloat16 [1024, 1024], P(None, 'dp'), may hold values from -0.1875 to 0.1875
- output_scale: bfloat16 [8, 1024], P(None, 'dp'), may hold values from 0.5 to 2
- widen_value: bfloat16 [1024, 2048], P(None, 'dp'), may hold values from -0.1875 to 0.1875
- widen_scale: bfloat16 [8, 2048], P(None, 'dp'), may hold values from 0.5 to 2
- narrow_value: bfloat16 [1024, 1024], P(None, 'dp'), may hold values from -0.1875 to 0.1875
- narrow_scale: bfloat16 [8, 1024], P(None, 'dp'), may hold values from 0.5 to 2
- kernel_taps: float32 [31, 1024], replicated, may hold values from -1 to 1
- gain_feed: float32 [1024], replicated, may hold values from 0.25 to 1.75
- gain_attend: float32 [1024], replicated, may hold values from 0.25 to 1.75
- gain_conv: float32 [1024], replicated, may hold values from 0.25 to 1.75
- gain_final: float32 [1024], replicated, may hold values from 0.25 to 1.75
- batch_scale: float32 [1024], replicated, may hold values from 0.5 to 2
- batch_shift: float32 [1024], replicated, may hold values from -3 to 3
Outputs:
- block_out: bfloat16 [8, 2048, 1024], P('dp', 'seq')
The draws below stay inside these ranges and needn't reach their ends.
Inputs may be any that keep to these rules, and one draw needn't show every extreme that they name: `project_scale`: block scales of the joined projection.
All inputs are finite; a program needn't handle non-finite values.
Results may differ from the reference program's by a relative error of at most 0.017.
The reference program's roundings to bfloat16 on the way count: a program that leaves them out, or rounds other values in their place, can miss the bound.
Values may be sent and summed in bfloat16 or wider, within the bound.
No kernel may reach another device: no remote copies, remote signals or barrier semaphores. Data moves between devices by JAX's collectives and lax.ppermute only.
A program may use at most 128 MiB of HBM per device.

```python
import math
import jax
import jax.numpy as jnp
from jax import lax

D = 1024
HEAD = 64
FF = 2816
KERNEL = 31
LENGTH = 2048
STREAMS = 8


def draw_tokens(key, part):
    base_key, row_key, col_key = jax.random.split(key, 3)
    shape_all = (STREAMS, LENGTH, D)
    base = jnp.clip(jax.random.normal(base_key, shape_all, jnp.float32), -5.0, 5.0)
    row_scale = jnp.exp(jax.random.uniform(row_key, (STREAMS, LENGTH, 1), jnp.float32, math.log(0.3), math.log(3.0)))
    col_scale = jnp.exp(jax.random.uniform(col_key, (1, 1, D), jnp.float32, math.log(0.3), math.log(3.0)))
    return (base * row_scale * col_scale).astype(jnp.bfloat16)


def draw_project_scale(key, part):
    low_key = jax.random.fold_in(key, 0)
    shape_all = (D // 128, 3 * D)
    drawn = jnp.exp(jax.random.uniform(low_key, shape_all, jnp.float32, math.log(0.5), math.log(2.0)))
    result = drawn
    return result.astype(jnp.bfloat16)


def levels(stream_key, extent, shards, smallest, high):
    factor_of, own = 1.0, jax.random.fold_in(stream_key, 6)
    for position, shards_of in shards:
        steps = jnp.exp(jax.random.uniform(jax.random.fold_in(own, position), (shards_of,), jnp.float32, smallest / len(shards), high / len(shards)))
        factor_of = factor_of * jnp.repeat(steps, extent[position] // shards_of).reshape([-1 if axis == position else 1 for axis in range(len(extent))])
    return factor_of


def normal_values(rng, shape, scale, bound, cuts=(), kind=jnp.bfloat16):
    array = scale * jax.random.normal(rng, shape, jnp.float32)
    if cuts:
        array = array * levels(rng, shape, cuts, -0.22, 0.18)
    return jnp.clip(array, -bound, bound).astype(kind)


def setup_inputs(seed: int = 0) -> dict:
    seeds = jax.random.split(jax.random.key(seed), 21)
    return {
        "tokens": draw_tokens(jax.random.fold_in(seeds[20], 71), 0),
        "expand_value": normal_values(seeds[1], (D, FF), D ** -0.5, 0.1875, ((1, 8),)),
        "expand_scale": jnp.clip(jnp.exp(math.log(2.0) - 1.3862944 * jax.random.uniform(seeds[2], (D // 128, FF), jnp.float32) ** levels(seeds[2], (D // 128, FF), ((1, 8),), -0.2, 0.2)), 0.5, 2.0).astype(jnp.bfloat16),
        "shrink_value": normal_values(seeds[3], (FF, D), FF ** -0.5, 0.109375, ((1, 8),)),
        "shrink_scale": jnp.clip(jnp.exp(math.log(2.0) - 1.3862944 * jax.random.uniform(seeds[4], (FF // 128, D), jnp.float32) ** levels(seeds[4], (FF // 128, D), ((1, 8),), -0.2, 0.2)), 0.5, 2.0).astype(jnp.bfloat16),
        "project_value": normal_values(seeds[5], (D, 3 * D), D ** -0.5, 0.1875, ((1, 8),)),
        "project_scale": draw_project_scale(jax.random.fold_in(seeds[20], 71), 0),
        "output_value": normal_values(seeds[7], (D, D), D ** -0.5, 0.1875, ((1, 8),)),
        "output_scale": jnp.clip(jnp.exp(math.log(2.0) - 1.3862944 * jax.random.uniform(seeds[8], (D // 128, D), jnp.float32) ** levels(seeds[8], (D // 128, D), ((1, 8),), -0.2, 0.2)), 0.5, 2.0).astype(jnp.bfloat16),
        "widen_value": normal_values(seeds[9], (D, 2 * D), D ** -0.5, 0.1875, ((1, 8),)),
        "widen_scale": jnp.clip(jnp.exp(math.log(2.0) - 1.3862944 * jax.random.uniform(seeds[10], (D // 128, 2 * D), jnp.float32) ** levels(seeds[10], (D // 128, 2 * D), ((1, 8),), -0.2, 0.2)), 0.5, 2.0).astype(jnp.bfloat16),
        "narrow_value": normal_values(seeds[11], (D, D), D ** -0.5, 0.1875, ((1, 8),)),
        "narrow_scale": jnp.clip(jnp.exp(math.log(2.0) - 1.3862944 * jax.random.uniform(seeds[12], (D // 128, D), jnp.float32) ** levels(seeds[12], (D // 128, D), ((1, 8),), -0.2, 0.2)), 0.5, 2.0).astype(jnp.bfloat16),
        "kernel_taps": normal_values(seeds[13], (KERNEL, D), KERNEL ** -0.5, 1.0, (), jnp.float32),
        "gain_feed": jnp.clip(1.0 + 0.15 * jax.random.normal(seeds[14], (D,), jnp.float32), 0.25, 1.75),
        "gain_attend": jnp.clip(1.0 + 0.15 * jax.random.normal(seeds[15], (D,), jnp.float32), 0.25, 1.75),
        "gain_conv": jnp.clip(1.0 + 0.15 * jax.random.normal(seeds[16], (D,), jnp.float32), 0.25, 1.75),
        "gain_final": jnp.clip(1.0 + 0.15 * jax.random.normal(seeds[17], (D,), jnp.float32), 0.25, 1.75),
        "batch_scale": jnp.clip(jnp.exp(jax.random.uniform(seeds[18], (D,), jnp.float32, math.log(0.5), math.log(2.0))), 0.5, 2.0),
        "batch_shift": normal_values(seeds[19], (D,), 0.5, 3.0, (), jnp.float32),
    }


def dequant(value_grid, scale_grid):
    stretched = jnp.repeat(scale_grid.astype(jnp.float32), 128, axis=0)
    return (value_grid.astype(jnp.float32) * stretched).astype(jnp.bfloat16)

def layer_norm(values, gain_row):
    average = lax.optimization_barrier(jnp.mean(values, axis=-1, keepdims=True))
    centred = values - average
    energy = lax.optimization_barrier(jnp.mean(centred * centred, axis=-1, keepdims=True))
    return centred * lax.rsqrt(energy + 1e-05) * gain_row

def attend(joined_heads, head_size):
    length = joined_heads.shape[0]
    head_count = joined_heads.shape[2] // head_size
    queries = joined_heads[:, 0].reshape(length, head_count, head_size)
    keys_all = joined_heads[:, 1].reshape(length, head_count, head_size).astype(jnp.float32)
    values_all = joined_heads[:, 2].reshape(length, head_count, head_size).astype(jnp.float32)
    block_rows = min(512, length)

    def one_block(query_rows):
        scores = jnp.einsum('qhd,khd->hqk', query_rows.astype(jnp.float32), keys_all) * head_size ** (-0.5)
        row_top = lax.optimization_barrier(jnp.max(scores, axis=-1, keepdims=True))
        raised = jnp.exp(scores - row_top)
        totals = lax.optimization_barrier(jnp.sum(raised, axis=-1, keepdims=True))
        weights_bf = raised.astype(jnp.bfloat16)
        mixed = jnp.einsum('hqk,khd->hqd', weights_bf.astype(jnp.float32), values_all) / totals
        return jnp.transpose(mixed, (1, 0, 2)).astype(jnp.bfloat16)
    blocks = queries.reshape(length // block_rows, block_rows, head_count, head_size)
    return lax.map(one_block, blocks).reshape(length, head_count * head_size)

def reference(tokens, expand_value, expand_scale, shrink_value, shrink_scale, project_value, project_scale, output_value, output_scale, widen_value, widen_scale, narrow_value, narrow_scale, kernel_taps, gain_feed, gain_attend, gain_conv, gain_final, batch_scale, batch_shift):
    expand_full = dequant(expand_value, expand_scale)
    shrink_full = dequant(shrink_value, shrink_scale)
    project_full = dequant(project_value, project_scale)
    output_full = dequant(output_value, output_scale)
    widen_full = dequant(widen_value, widen_scale)
    narrow_full = dequant(narrow_value, narrow_scale)
    model_width = D
    half_taps = KERNEL // 2

    def one_stream(stream):
        length = stream.shape[0]
        residual_in = stream.astype(jnp.float32)
        feed_in = layer_norm(residual_in, gain_feed).astype(jnp.bfloat16)
        hidden = jax.nn.silu(jnp.dot(feed_in, expand_full, preferred_element_type=jnp.float32)).astype(jnp.bfloat16)
        after_feed = residual_in + 0.5 * jnp.dot(hidden, shrink_full, preferred_element_type=jnp.float32)
        attend_in = layer_norm(after_feed, gain_attend).astype(jnp.bfloat16)
        joined_heads = jnp.dot(attend_in, project_full, preferred_element_type=jnp.float32).astype(jnp.bfloat16)
        joined_heads = joined_heads.reshape(length, 3, model_width)
        context = attend(joined_heads, HEAD)
        after_attend = after_feed + jnp.dot(context, output_full, preferred_element_type=jnp.float32)
        conv_in = layer_norm(after_attend, gain_conv).astype(jnp.bfloat16)
        widened = jnp.dot(conv_in, widen_full, preferred_element_type=jnp.float32)
        gated_rows = (widened[:, :model_width] * jax.nn.sigmoid(widened[:, model_width:])).astype(jnp.bfloat16)
        padded = jnp.pad(gated_rows, ((half_taps, half_taps), (0, 0)))
        filtered = jnp.zeros((length, model_width), jnp.float32)
        for offset in range(KERNEL):
            filtered = filtered + kernel_taps[offset] * padded[offset:offset + length].astype(jnp.float32)
        activated = jax.nn.silu(filtered * batch_scale + batch_shift).astype(jnp.bfloat16)
        after_conv = after_attend + jnp.dot(activated, narrow_full, preferred_element_type=jnp.float32)
        return layer_norm(after_conv, gain_final).astype(jnp.bfloat16)
    return lax.map(one_stream, tokens)
```

```python
import functools
import math

import jax
import jax.numpy as jnp
from jax import lax
from jax.experimental import pallas as pl
from jax.experimental.pallas import tpu as pltpu
from jax.sharding import PartitionSpec as P

HEAD = 64
KERNEL = 31
LANES = 128
HALO = 16
NT = (((1,), (1,)), ((), ()))


def dequant(value_grid, scale_grid):
    stretched = jnp.repeat(scale_grid.astype(jnp.float32), 128, axis=0)
    return (value_grid.astype(jnp.float32) * stretched).astype(jnp.bfloat16)


def own_rows_of(value_grid, scale_grid):
    return jnp.transpose(dequant(value_grid, scale_grid))


def gathered(rows):
    return lax.all_gather(rows, "dp", axis=0, tiled=True)


def product(left, right):
    return lax.dot_general(left, right, NT, preferred_element_type=jnp.float32)


def layer_norm(values, gain_row):
    average = jnp.mean(values, axis=-1, keepdims=True)
    centred = values - average
    energy = jnp.mean(centred * centred, axis=-1, keepdims=True)
    return centred * lax.rsqrt(energy + 1e-05) * gain_row


def attention_kernel(count, tile, q_ref, *refs):
    keys, values, out_ref = refs[:count], refs[count : 2 * count], refs[2 * count]
    rows = q_ref.shape[0]
    heads = LANES // HEAD
    lane = lax.broadcasted_iota(jnp.int32, (tile, LANES), 1) // HEAD
    factor = HEAD ** (-0.5) * math.log2(math.e)
    tiles = [(start, head) for start in range(0, rows, tile) for head in range(heads)]

    def scores_of(start, head):
        picked = jnp.where(lane == head, q_ref[start : start + tile, :], jnp.bfloat16(0))
        return [
            lax.dot_general(picked, k[...], NT, preferred_element_type=jnp.float32) for k in keys
        ]

    def context_of(scores):
        top = functools.reduce(jnp.maximum, [jnp.max(s, axis=1, keepdims=True) for s in scores])
        raised = [jnp.exp2((s - top) * factor) for s in scores]
        totals = sum(jnp.sum(r, axis=1, keepdims=True) for r in raised)
        mixed = sum(
            jnp.dot(r.astype(jnp.bfloat16), v[...], preferred_element_type=jnp.float32)
            for r, v in zip(raised, values)
        )
        return mixed / totals

    pending = scores_of(*tiles[0])
    merged = None
    for index, (start, head) in enumerate(tiles):
        scores = pending
        if index + 1 < len(tiles):
            pending = scores_of(*tiles[index + 1])
        mixed = context_of(scores)
        merged = mixed if head == 0 else jnp.where(lane == head, mixed, merged)
        if head == heads - 1:
            out_ref[start : start + tile, :] = merged.astype(jnp.bfloat16)


def attention(queries, pairs):
    rows, width = queries.shape
    count = len(pairs)
    length = sum(p.shape[0] for p in pairs)
    steps = width // LANES
    spec = pl.BlockSpec((rows, LANES), lambda h: (0, h))
    return pl.pallas_call(
        functools.partial(attention_kernel, count, min(256, rows)),
        grid=(steps,),
        out_shape=jax.ShapeDtypeStruct((rows, width), jnp.bfloat16),
        in_specs=[spec]
        + [pl.BlockSpec((p.shape[0], LANES), lambda h: (0, h)) for p in pairs]
        + [pl.BlockSpec((p.shape[0], LANES), lambda h: (0, h + steps)) for p in pairs],
        out_specs=spec,
        compiler_params=pltpu.CompilerParams(vmem_limit_bytes=40 << 20),
        cost_estimate=pl.CostEstimate(
            flops=16 * rows * length * width,
            bytes_accessed=4 * (rows + length) * width,
            transcendentals=rows * length * width // HEAD,
        ),
        name="attention",
    )(queries, *pairs, *pairs)


def conv_kernel(gated_ref, before_ref, after_ref, taps_ref, scale_ref, shift_ref, out_ref, padded, shifted):
    rows = gated_ref.shape[0]
    total = rows + 2 * HALO
    padded[0:HALO, :] = before_ref[...].astype(jnp.float32)
    padded[HALO : HALO + rows, :] = gated_ref[...].astype(jnp.float32)
    padded[HALO + rows : total, :] = after_ref[...].astype(jnp.float32)
    lead = HALO - KERNEL // 2
    for residue in range(1, 8):
        shifted[residue, 0 : total - 8, :] = padded[residue : residue + total - 8, :]
    tile = min(128, rows)
    for start in range(0, rows, tile):
        filtered = jnp.zeros((tile, LANES), jnp.float32)
        for tap in range(KERNEL):
            offset = tap + lead
            base = start + offset // 8 * 8
            if offset % 8 == 0:
                piece = padded[base : base + tile, :]
            else:
                piece = shifted[offset % 8, base : base + tile, :]
            filtered = filtered + taps_ref[tap : tap + 1, :] * piece
        moved = filtered * scale_ref[...] + shift_ref[...]
        out_ref[start : start + tile, :] = (moved / (1.0 + jnp.exp(-moved))).astype(jnp.bfloat16)


def convolved(gated, before, after, taps, scale, shift):
    rows, width = gated.shape
    total = rows + 2 * HALO
    return pl.pallas_call(
        conv_kernel,
        grid=(width // LANES,),
        out_shape=jax.ShapeDtypeStruct((rows, width), jnp.bfloat16),
        in_specs=[
            pl.BlockSpec((rows, LANES), lambda c: (0, c)),
            pl.BlockSpec((HALO, LANES), lambda c: (0, c)),
            pl.BlockSpec((HALO, LANES), lambda c: (0, c)),
            pl.BlockSpec((KERNEL, LANES), lambda c: (0, c)),
            pl.BlockSpec((1, LANES), lambda c: (0, c)),
            pl.BlockSpec((1, LANES), lambda c: (0, c)),
        ],
        out_specs=pl.BlockSpec((rows, LANES), lambda c: (0, c)),
        scratch_shapes=[
            pltpu.VMEM((total, LANES), jnp.float32),
            pltpu.VMEM((8, total, LANES), jnp.float32),
        ],
        compiler_params=pltpu.CompilerParams(vmem_limit_bytes=32 << 20),
        cost_estimate=pl.CostEstimate(
            flops=2 * KERNEL * rows * width, bytes_accessed=4 * rows * width, transcendentals=rows * width
        ),
        name="conv",
    )(gated, before, after, taps, scale[None], shift[None])


def body(
    tokens,
    expand_value,
    expand_scale,
    shrink_value,
    shrink_scale,
    project_value,
    project_scale,
    output_value,
    output_scale,
    widen_value,
    widen_scale,
    narrow_value,
    narrow_scale,
    kernel_taps,
    gain_feed,
    gain_attend,
    gain_conv,
    gain_final,
    batch_scale,
    batch_shift,
):
    width = tokens.shape[2]
    count = lax.axis_size("seq")
    ring = [(i, (i + 1) % count) for i in range(count)]
    chunks = [tokens[0]]
    for _ in range(count - 1):
        chunks.append(lax.ppermute(chunks[-1], "seq", ring))
    expand_full = gathered(own_rows_of(expand_value, expand_scale))
    shrink_full = gathered(own_rows_of(shrink_value, shrink_scale))
    project_full = gathered(own_rows_of(project_value, project_scale))
    tail = [
        own_rows_of(output_value, output_scale),
        own_rows_of(widen_value, widen_scale),
        own_rows_of(narrow_value, narrow_scale),
    ]
    tail_all = lax.all_gather(jnp.concatenate(tail, axis=0), "dp", axis=0)
    marks = [0]
    for part in tail:
        marks.append(marks[-1] + part.shape[0])
    output_full, widen_full, narrow_full = (
        tail_all[:, a:b].reshape(-1, width) for a, b in zip(marks[:-1], marks[1:])
    )

    after_feed, pairs, queries = None, [], None
    for index, chunk in enumerate(chunks):
        residual_in = chunk.astype(jnp.float32)
        feed_in = layer_norm(residual_in, gain_feed).astype(jnp.bfloat16)
        hidden = jax.nn.silu(product(feed_in, expand_full)).astype(jnp.bfloat16)
        fed = residual_in + 0.5 * product(hidden, shrink_full)
        attend_in = layer_norm(fed, gain_attend).astype(jnp.bfloat16)
        pairs.append(product(attend_in, project_full[width:]).astype(jnp.bfloat16))
        if index == 0:
            after_feed = fed
            queries = product(attend_in, project_full[:width]).astype(jnp.bfloat16)
    context = attention(queries, pairs)
    after_attend = after_feed + product(context, output_full)
    conv_in = layer_norm(after_attend, gain_conv).astype(jnp.bfloat16)
    widened = product(conv_in, widen_full)
    gated = (widened[:, :width] * jax.nn.sigmoid(widened[:, width:])).astype(jnp.bfloat16)
    before = lax.ppermute(gated[-HALO:], "seq", [(i, i + 1) for i in range(count - 1)])
    after = lax.ppermute(gated[:HALO], "seq", [(i + 1, i) for i in range(count - 1)])
    activated = convolved(gated, before, after, kernel_taps, batch_scale, batch_shift)
    after_conv = after_attend + product(activated, narrow_full)
    return layer_norm(after_conv, gain_final).astype(jnp.bfloat16)[None]


def solution(mesh):
    weights = (P(None, "dp"),) * 12
    return jax.shard_map(
        body,
        mesh=mesh,
        in_specs=(P("dp", "seq", None),) + weights + (P(),) * 7,
        out_specs=P("dp", "seq", None),
        check_vma=False,
    )
```

```python
import functools
import math

import jax
import jax.numpy as jnp
from jax import lax
from jax.experimental import pallas as pl
from jax.experimental.pallas import tpu as pltpu
from jax.sharding import PartitionSpec as P

HEAD = 64
KERNEL = 31
LANES = 128
HALO = 16
NT = (((1,), (1,)), ((), ()))


def dequant(value_grid, scale_grid):
    stretched = jnp.repeat(scale_grid.astype(jnp.float32), 128, axis=0)
    return (value_grid.astype(jnp.float32) * stretched).astype(jnp.bfloat16)


def own_rows_of(value_grid, scale_grid):
    return jnp.transpose(dequant(value_grid, scale_grid))


def gathered(rows):
    return lax.all_gather(rows, "dp", axis=0, tiled=True)


def product(left, right):
    return lax.dot_general(left, right, NT, preferred_element_type=jnp.float32)


def layer_norm(values, gain_row):
    average = jnp.mean(values, axis=-1, keepdims=True)
    centred = values - average
    energy = jnp.mean(centred * centred, axis=-1, keepdims=True)
    return centred * lax.rsqrt(energy + 1e-05) * gain_row


def partners(size, bit):
    return [(i, i ^ bit) for i in range(size)]


def exchanged(parts):
    size = lax.axis_size("dp")
    bits = [1 << b for b in range(1, size.bit_length() - 1)]
    found = []
    for number, part in enumerate(parts):
        held = [(0, part)]
        for bit in bits if number % 2 == 0 else bits[::-1]:
            held += [(far ^ bit, lax.ppermute(a, "dp", partners(size, bit))) for far, a in held]
        held += [(far ^ 1, lax.ppermute(a, "dp", partners(size, 1))) for far, a in held]
        found += [(far, number, a) for far, a in held]
    return found


def copies(pieces, refs, target, sems, share):
    own = lax.axis_index("dp")
    made = []
    for index, ((far, number), ref) in enumerate(zip(pieces, refs)):
        start = (own ^ far) * share + number * ref.shape[0]
        start = pl.multiple_of(start, 16)
        made.append(
            pltpu.make_async_copy(ref, target.at[pl.ds(start, ref.shape[0]), :], sems.at[index])
        )
    return made


def kernel_norm(values, gain_row):
    scale = 1.0 / values.shape[1]
    average = jnp.sum(values, axis=1, keepdims=True) * scale
    centred = values - average
    energy = jnp.sum(centred * centred, axis=1, keepdims=True) * scale
    return centred * lax.rsqrt(energy + 1e-05) * gain_row


def silu(v):
    half = 0.5 * v
    return half + half * jnp.tanh(half)


def feed_kernel(chunks, pieces, share, *refs):
    refs = list(refs)
    tokens = [refs.pop(0) for _ in range(chunks)]
    gain_feed, gain_attend, expand = refs.pop(0), refs.pop(0), refs.pop(0)
    shrink_refs = [refs.pop(0) for _ in pieces]
    attend_in, fed, held, expand_all, shrink_all, feed_in, hidden, total = refs[:8]
    token_sems, expand_sems, shrink_sems = refs[8:]
    step = pl.program_id(0)
    units, width = expand_all.shape
    block = 256

    token_copies = [
        pltpu.make_async_copy(t, held.at[i], token_sems.at[i]) for i, t in enumerate(tokens)
    ]
    expand_copies = [
        pltpu.make_async_copy(
            expand.at[pl.ds(n * block, block), :],
            expand_all.at[pl.ds(n * block, block), :],
            expand_sems.at[n],
        )
        for n in range(units // block)
    ]
    shrink_copies = copies(pieces, shrink_refs, shrink_all, shrink_sems, share)

    @pl.when(step == 0)
    def _():
        for copy in token_copies[:1] + expand_copies + shrink_copies + token_copies[1:]:
            copy.start()

    for i in range(chunks):
        @pl.when(step == i)
        def _(i=i):
            token_copies[i].wait()

    feed_in[...] = kernel_norm(held[step].astype(jnp.float32), gain_feed[...]).astype(jnp.bfloat16)

    @pl.when(step == 0)
    def _():
        for copy in expand_copies:
            copy.wait()

    for n in range(units // block):
        piece = slice(n * block, (n + 1) * block)
        hidden[:, piece] = silu(product(feed_in[...], expand_all[piece, :])).astype(jnp.bfloat16)

    @pl.when(step == 0)
    def _():
        for copy in shrink_copies:
            copy.wait()

    for n in range(width // block):
        piece = slice(n * block, (n + 1) * block)
        total[:, piece] = held[step, :, piece].astype(jnp.float32) + 0.5 * product(
            hidden[...], shrink_all[piece, :]
        )
    attend_in[...] = kernel_norm(total[...], gain_attend[...]).astype(jnp.bfloat16)

    @pl.when(step == 0)
    def _():
        fed[...] = total[...]


def feed(chunks, gain_feed, gain_attend, expand_full, shrink_pieces):
    rows, width = chunks[0].shape
    units = expand_full.shape[0]
    count = len(chunks)
    anywhere = pl.BlockSpec(memory_space=pl.ANY)
    row = pl.BlockSpec((1, width), lambda i: (0, 0))
    share = width // lax.axis_size("dp")
    return pl.pallas_call(
        functools.partial(feed_kernel, count, [p[:2] for p in shrink_pieces], share),
        grid=(count,),
        out_shape=[
            jax.ShapeDtypeStruct((count * rows, width), jnp.bfloat16),
            jax.ShapeDtypeStruct((rows, width), jnp.float32),
        ],
        in_specs=[anywhere] * count + [row, row, anywhere] + [anywhere] * len(shrink_pieces),
        out_specs=[
            pl.BlockSpec((rows, width), lambda i: (i, 0)),
            pl.BlockSpec((rows, width), lambda i: (0, 0)),
        ],
        scratch_shapes=[
            pltpu.VMEM((count, rows, width), jnp.bfloat16),
            pltpu.VMEM((units, width), jnp.bfloat16),
            pltpu.VMEM((width, units), jnp.bfloat16),
            pltpu.VMEM((rows, width), jnp.bfloat16),
            pltpu.VMEM((rows, units), jnp.bfloat16),
            pltpu.VMEM((rows, width), jnp.float32),
            pltpu.SemaphoreType.DMA((count,)),
            pltpu.SemaphoreType.DMA((units // 256,)),
            pltpu.SemaphoreType.DMA((len(shrink_pieces),)),
        ],
        compiler_params=pltpu.CompilerParams(vmem_limit_bytes=48 << 20),
        cost_estimate=pl.CostEstimate(
            flops=4 * count * rows * width * units,
            bytes_accessed=4 * units * width + 4 * count * rows * width,
            transcendentals=count * rows * units,
        ),
        name="feed",
    )(
        *chunks, gain_feed[None], gain_attend[None], expand_full, *[p[2] for p in shrink_pieces]
    )


def project_kernel(inputs, pieces, share, *refs):
    refs = list(refs)
    sources = [refs.pop(0) for _ in range(inputs)]
    weight_refs = [refs.pop(0) for _ in pieces]
    queries = refs.pop(0)
    pairs = [refs.pop(0) for _ in range(inputs)]
    weights, sems = refs
    step = pl.program_id(0)
    rows, block = queries.shape
    made = copies(pieces, weight_refs, weights, sems, share)

    @pl.when(step == 0)
    def _():
        for copy in made:
            copy.start()
        for copy in made:
            copy.wait()

    piece = weights[pl.ds(pl.multiple_of(step * block, block), block), :]
    parts = weights.shape[1] // block

    @pl.when(step < parts)
    def _():
        queries[...] = product(sources[0][:rows, :], piece).astype(jnp.bfloat16)

    @pl.when(step >= parts)
    def _():
        for source, pair in zip(sources, pairs):
            for start in range(0, source.shape[0], rows):
                pair[start : start + rows, :] = product(
                    source[start : start + rows, :], piece
                ).astype(jnp.bfloat16)


def projected(sources, rows, pieces):
    width = sources[0].shape[1]
    block = 256
    parts = width // block
    share = 3 * width // lax.axis_size("dp")
    length = sum(s.shape[0] for s in sources)
    anywhere = pl.BlockSpec(memory_space=pl.ANY)
    return pl.pallas_call(
        functools.partial(project_kernel, len(sources), [p[:2] for p in pieces], share),
        grid=(3 * parts,),
        out_shape=[jax.ShapeDtypeStruct((rows, width), jnp.bfloat16)]
        + [jax.ShapeDtypeStruct((s.shape[0], 2 * width), jnp.bfloat16) for s in sources],
        in_specs=[pl.BlockSpec(s.shape, lambda i: (0, 0)) for s in sources]
        + [anywhere] * len(pieces),
        out_specs=[pl.BlockSpec((rows, block), lambda i: (0, jnp.minimum(i, parts - 1)))]
        + [
            pl.BlockSpec((s.shape[0], block), lambda i: (0, jnp.maximum(i - parts, 0)))
            for s in sources
        ],
        scratch_shapes=[
            pltpu.VMEM((3 * width, width), jnp.bfloat16),
            pltpu.SemaphoreType.DMA((len(pieces),)),
        ],
        compiler_params=pltpu.CompilerParams(vmem_limit_bytes=56 << 20),
        cost_estimate=pl.CostEstimate(
            flops=2 * width * width * (rows + 2 * length),
            bytes_accessed=2 * width * (3 * width + rows + 3 * length),
            transcendentals=0,
        ),
        name="project",
    )(*sources, *[p[2] for p in pieces])


def attention_kernel(count, tile, q_ref, *refs):
    keys, values, out_ref = refs[:count], refs[count : 2 * count], refs[2 * count]
    rows = q_ref.shape[0]
    heads = LANES // HEAD
    lane = lax.broadcasted_iota(jnp.int32, (tile, LANES), 1) // HEAD
    factor = HEAD ** (-0.5) * math.log2(math.e)
    tiles = [(start, head) for start in range(0, rows, tile) for head in range(heads)]

    def scores_of(start, head):
        picked = jnp.where(lane == head, q_ref[start : start + tile, :], jnp.bfloat16(0))
        return [
            lax.dot_general(picked, k[...], NT, preferred_element_type=jnp.float32) for k in keys
        ]

    def context_of(scores):
        top = functools.reduce(jnp.maximum, [jnp.max(s, axis=1, keepdims=True) for s in scores])
        raised = [jnp.exp2((s - top) * factor) for s in scores]
        totals = sum(jnp.sum(r, axis=1, keepdims=True) for r in raised)
        mixed = sum(
            jnp.dot(r.astype(jnp.bfloat16), v[...], preferred_element_type=jnp.float32)
            for r, v in zip(raised, values)
        )
        return mixed / totals

    pending = scores_of(*tiles[0])
    merged = None
    for index, (start, head) in enumerate(tiles):
        scores = pending
        if index + 1 < len(tiles):
            pending = scores_of(*tiles[index + 1])
        mixed = context_of(scores)
        merged = mixed if head == 0 else jnp.where(lane == head, mixed, merged)
        if head == heads - 1:
            out_ref[start : start + tile, :] = merged.astype(jnp.bfloat16)


def attention(queries, pairs):
    rows, width = queries.shape
    count = len(pairs)
    length = sum(p.shape[0] for p in pairs)
    steps = width // LANES
    spec = pl.BlockSpec((rows, LANES), lambda h: (0, h))
    return pl.pallas_call(
        functools.partial(attention_kernel, count, min(256, rows)),
        grid=(steps,),
        out_shape=jax.ShapeDtypeStruct((rows, width), jnp.bfloat16),
        in_specs=[spec]
        + [pl.BlockSpec((p.shape[0], LANES), lambda h: (0, h)) for p in pairs]
        + [pl.BlockSpec((p.shape[0], LANES), lambda h: (0, h + steps)) for p in pairs],
        out_specs=spec,
        compiler_params=pltpu.CompilerParams(vmem_limit_bytes=40 << 20),
        cost_estimate=pl.CostEstimate(
            flops=16 * rows * length * width,
            bytes_accessed=4 * (rows + length) * width,
            transcendentals=rows * length * width // HEAD,
        ),
        name="attention",
    )(queries, *pairs, *pairs)


def conv_kernel(gated_ref, before_ref, after_ref, taps_ref, scale_ref, shift_ref, out_ref, padded, shifted):
    rows = gated_ref.shape[0]
    total = rows + 2 * HALO
    padded[0:HALO, :] = before_ref[...].astype(jnp.float32)
    padded[HALO : HALO + rows, :] = gated_ref[...].astype(jnp.float32)
    padded[HALO + rows : total, :] = after_ref[...].astype(jnp.float32)
    lead = HALO - KERNEL // 2
    for residue in range(1, 8):
        shifted[residue, 0 : total - 8, :] = padded[residue : residue + total - 8, :]
    tile = min(128, rows)
    for start in range(0, rows, tile):
        filtered = jnp.zeros((tile, LANES), jnp.float32)
        for tap in range(KERNEL):
            offset = tap + lead
            base = start + offset // 8 * 8
            if offset % 8 == 0:
                piece = padded[base : base + tile, :]
            else:
                piece = shifted[offset % 8, base : base + tile, :]
            filtered = filtered + taps_ref[tap : tap + 1, :] * piece
        moved = filtered * scale_ref[...] + shift_ref[...]
        out_ref[start : start + tile, :] = (moved / (1.0 + jnp.exp(-moved))).astype(jnp.bfloat16)


def convolved(gated, before, after, taps, scale, shift):
    rows, width = gated.shape
    total = rows + 2 * HALO
    return pl.pallas_call(
        conv_kernel,
        grid=(width // LANES,),
        out_shape=jax.ShapeDtypeStruct((rows, width), jnp.bfloat16),
        in_specs=[
            pl.BlockSpec((rows, LANES), lambda c: (0, c)),
            pl.BlockSpec((HALO, LANES), lambda c: (0, c)),
            pl.BlockSpec((HALO, LANES), lambda c: (0, c)),
            pl.BlockSpec((KERNEL, LANES), lambda c: (0, c)),
            pl.BlockSpec((1, LANES), lambda c: (0, c)),
            pl.BlockSpec((1, LANES), lambda c: (0, c)),
        ],
        out_specs=pl.BlockSpec((rows, LANES), lambda c: (0, c)),
        scratch_shapes=[
            pltpu.VMEM((total, LANES), jnp.float32),
            pltpu.VMEM((8, total, LANES), jnp.float32),
        ],
        compiler_params=pltpu.CompilerParams(vmem_limit_bytes=32 << 20),
        cost_estimate=pl.CostEstimate(
            flops=2 * KERNEL * rows * width, bytes_accessed=4 * rows * width, transcendentals=rows * width
        ),
        name="conv",
    )(gated, before, after, taps, scale[None], shift[None])


def body(
    tokens,
    expand_value,
    expand_scale,
    shrink_value,
    shrink_scale,
    project_value,
    project_scale,
    output_value,
    output_scale,
    widen_value,
    widen_scale,
    narrow_value,
    narrow_scale,
    kernel_taps,
    gain_feed,
    gain_attend,
    gain_conv,
    gain_final,
    batch_scale,
    batch_shift,
):
    width = tokens.shape[2]
    count = lax.axis_size("seq")
    ring = [(i, (i + 1) % count) for i in range(count)]
    chunks = [tokens[0]]
    for _ in range(count - 1):
        chunks.append(lax.ppermute(chunks[-1], "seq", ring))
    expand_full = gathered(own_rows_of(expand_value, expand_scale))
    shrink_pieces = exchanged(jnp.split(own_rows_of(shrink_value, shrink_scale), 2))
    project_parts = jnp.split(own_rows_of(project_value, project_scale), 2)
    last, *project_parts = lax.optimization_barrier((shrink_pieces[-1][2], *project_parts))
    shrink_pieces[-1] = (*shrink_pieces[-1][:2], last)
    project_pieces = exchanged(project_parts)
    tail = [
        own_rows_of(output_value, output_scale),
        own_rows_of(widen_value, widen_scale),
        own_rows_of(narrow_value, narrow_scale),
    ]
    tail_all = lax.all_gather(jnp.concatenate(tail, axis=0), "dp", axis=0)
    marks = [0]
    for part in tail:
        marks.append(marks[-1] + part.shape[0])
    output_full, widen_full, narrow_full = (
        tail_all[:, a:b].reshape(-1, width) for a, b in zip(marks[:-1], marks[1:])
    )

    attend_near, after_feed = feed(
        chunks[:-1], gain_feed, gain_attend, expand_full, shrink_pieces
    )
    attend_far, _ = feed(chunks[-1:], gain_feed, gain_attend, expand_full, shrink_pieces)
    queries, *pairs = projected([attend_near, attend_far], chunks[0].shape[0], project_pieces)
    context = attention(queries, pairs)
    after_attend = after_feed + product(context, output_full)
    conv_in = layer_norm(after_attend, gain_conv).astype(jnp.bfloat16)
    widened = product(conv_in, widen_full)
    gated = (widened[:, :width] * jax.nn.sigmoid(widened[:, width:])).astype(jnp.bfloat16)
    before = lax.ppermute(gated[-HALO:], "seq", [(i, i + 1) for i in range(count - 1)])
    after = lax.ppermute(gated[:HALO], "seq", [(i + 1, i) for i in range(count - 1)])
    activated = convolved(gated, before, after, kernel_taps, batch_scale, batch_shift)
    after_conv = after_attend + product(activated, narrow_full)
    return layer_norm(after_conv, gain_final).astype(jnp.bfloat16)[None]


def solution(mesh):
    weights = (P(None, "dp"),) * 12
    return jax.shard_map(
        body,
        mesh=mesh,
        in_specs=(P("dp", "seq", None),) + weights + (P(),) * 7,
        out_specs=P("dp", "seq", None),
        check_vma=False,
    )
```

```python
import functools
import math

import jax
import jax.numpy as jnp
from jax import lax
from jax.experimental import pallas as pl
from jax.experimental.pallas import tpu as pltpu
from jax.sharding import PartitionSpec as P

HEAD = 64
KERNEL = 31
LANES = 128
HALO = 16
NT = (((1,), (1,)), ((), ()))


def dequant(value_grid, scale_grid):
    stretched = jnp.repeat(scale_grid.astype(jnp.float32), 128, axis=0)
    return (value_grid.astype(jnp.float32) * stretched).astype(jnp.bfloat16)


def own_rows_of(value_grid, scale_grid):
    return jnp.transpose(dequant(value_grid, scale_grid))


def gathered(rows):
    return lax.all_gather(rows, "dp", axis=0, tiled=True)


def product(left, right):
    return lax.dot_general(left, right, NT, preferred_element_type=jnp.float32)


def layer_norm(values, gain_row):
    average = jnp.mean(values, axis=-1, keepdims=True)
    centred = values - average
    energy = jnp.mean(centred * centred, axis=-1, keepdims=True)
    return centred * lax.rsqrt(energy + 1e-05) * gain_row


def partners(size, bit):
    return [(i, i ^ bit) for i in range(size)]


def send(array, bit):
    return lax.ppermute(array, "dp", partners(lax.axis_size("dp"), bit))


def far_bits():
    return [1 << b for b in range(1, lax.axis_size("dp").bit_length() - 1)]


def stage(held, bit):
    return held + [(far ^ bit, number, send(a, bit)) for far, number, a in held]


def first_stages(parts):
    bits = far_bits()
    return [
        ([(0, number, part)], [(bit, number, send(part, bit)) for bit in bits])
        for number, part in enumerate(parts)
    ]


def later_stages(sets):
    bits = far_bits()
    result = []
    for own, first in sets:
        number = own[0][1]
        order = bits if number % 2 == 0 else bits[::-1]
        by_bit = dict(zip(bits, first))
        held = list(own)
        for bit in order:
            held += [by_bit[bit]] + [(far ^ bit, n, send(a, bit)) for far, n, a in held[1:]]
        result += held
    return result


def crossed(held):
    return stage(held, 1)


def refilled(sets, arrays):
    arrays = list(arrays)
    return [
        tuple([(far, n, arrays.pop(0)) for far, n, _ in group] for group in pair) for pair in sets
    ]


def barrier(*trees):
    return lax.optimization_barrier(trees)


def copies(pieces, refs, target, sems, share):
    own = lax.axis_index("dp")
    made = []
    for index, ((far, number), ref) in enumerate(zip(pieces, refs)):
        start = (own ^ far) * share + number * ref.shape[0]
        start = pl.multiple_of(start, 16)
        made.append(
            pltpu.make_async_copy(ref, target.at[pl.ds(start, ref.shape[0]), :], sems.at[index])
        )
    return made


def kernel_norm(values, gain_row):
    scale = 1.0 / values.shape[1]
    average = jnp.sum(values, axis=1, keepdims=True) * scale
    centred = values - average
    energy = jnp.sum(centred * centred, axis=1, keepdims=True) * scale
    return centred * lax.rsqrt(energy + 1e-05) * gain_row


def silu(v):
    half = 0.5 * v
    return half + half * jnp.tanh(half)


def feed_kernel(chunks, pieces, share, edge, *refs):
    refs = list(refs)
    tokens = [refs.pop(0) for _ in range(chunks)]
    gain_feed, gain_attend, expand = refs.pop(0), refs.pop(0), refs.pop(0)
    shrink_refs = [refs.pop(0) for _ in pieces]
    attend_in, fed, fed_edge, held, expand_all, shrink_all, feed_in, hidden, total = refs[:9]
    token_sems, expand_sems, shrink_sems = refs[9:]
    step = pl.program_id(0)
    units, width = expand_all.shape
    block = 256

    token_copies = [
        pltpu.make_async_copy(t, held.at[i], token_sems.at[i]) for i, t in enumerate(tokens)
    ]
    expand_copies = [
        pltpu.make_async_copy(
            expand.at[pl.ds(n * block, block), :],
            expand_all.at[pl.ds(n * block, block), :],
            expand_sems.at[n],
        )
        for n in range(units // block)
    ]
    shrink_copies = copies(pieces, shrink_refs, shrink_all, shrink_sems, share)

    @pl.when(step == 0)
    def _():
        for copy in token_copies[:1] + expand_copies + shrink_copies + token_copies[1:]:
            copy.start()

    for i in range(chunks):
        @pl.when(step == i)
        def _(i=i):
            token_copies[i].wait()

    feed_in[...] = kernel_norm(held[step].astype(jnp.float32), gain_feed[...]).astype(jnp.bfloat16)

    @pl.when(step == 0)
    def _():
        for copy in expand_copies:
            copy.wait()

    for n in range(units // block):
        piece = slice(n * block, (n + 1) * block)
        hidden[:, piece] = silu(product(feed_in[...], expand_all[piece, :])).astype(jnp.bfloat16)

    @pl.when(step == 0)
    def _():
        for copy in shrink_copies:
            copy.wait()

    for n in range(width // block):
        piece = slice(n * block, (n + 1) * block)
        total[:, piece] = held[step, :, piece].astype(jnp.float32) + 0.5 * product(
            hidden[...], shrink_all[piece, :]
        )
    attend_in[...] = kernel_norm(total[...], gain_attend[...]).astype(jnp.bfloat16)

    @pl.when(step == 0)
    def _():
        fed[...] = total[...]

    @pl.when(step == edge[0])
    def _():
        fed_edge[...] = total[edge[1] : edge[1] + HALO, :]


def feed(chunks, edge, gain_feed, gain_attend, expand_full, shrink_pieces):
    rows, width = chunks[0].shape
    units = expand_full.shape[0]
    count = len(chunks)
    anywhere = pl.BlockSpec(memory_space=pltpu.HBM)
    row = pl.BlockSpec((1, width), lambda i: (0, 0))
    share = width // lax.axis_size("dp")
    return pl.pallas_call(
        functools.partial(feed_kernel, count, [p[:2] for p in shrink_pieces], share, edge),
        grid=(count,),
        out_shape=[
            jax.ShapeDtypeStruct((count * rows, width), jnp.bfloat16),
            jax.ShapeDtypeStruct((rows, width), jnp.float32),
            jax.ShapeDtypeStruct((HALO, width), jnp.float32),
        ],
        in_specs=[anywhere] * count + [row, row, anywhere] + [anywhere] * len(shrink_pieces),
        out_specs=[
            pl.BlockSpec((rows, width), lambda i: (i, 0)),
            pl.BlockSpec((rows, width), lambda i: (0, 0)),
            pl.BlockSpec((HALO, width), lambda i: (0, 0)),
        ],
        scratch_shapes=[
            pltpu.VMEM((count, rows, width), jnp.bfloat16),
            pltpu.VMEM((units, width), jnp.bfloat16),
            pltpu.VMEM((width, units), jnp.bfloat16),
            pltpu.VMEM((rows, width), jnp.bfloat16),
            pltpu.VMEM((rows, units), jnp.bfloat16),
            pltpu.VMEM((rows, width), jnp.float32),
            pltpu.SemaphoreType.DMA((count,)),
            pltpu.SemaphoreType.DMA((units // 256,)),
            pltpu.SemaphoreType.DMA((len(shrink_pieces),)),
        ],
        compiler_params=pltpu.CompilerParams(vmem_limit_bytes=48 << 20),
        cost_estimate=pl.CostEstimate(
            flops=4 * count * rows * width * units,
            bytes_accessed=4 * units * width + 4 * count * rows * width,
            transcendentals=count * rows * units,
        ),
        name="feed",
    )(
        *chunks, gain_feed[None], gain_attend[None], expand_full, *[p[2] for p in shrink_pieces]
    )


def project_kernel(inputs, pieces, share, *refs):
    refs = list(refs)
    query_source = refs.pop(0)
    sources = [refs.pop(0) for _ in range(inputs)]
    weight_refs = [refs.pop(0) for _ in pieces]
    queries = refs.pop(0)
    pairs = [refs.pop(0) for _ in range(inputs)]
    weights, sems = refs
    step = pl.program_id(0)
    block = queries.shape[1]
    made = copies(pieces, weight_refs, weights, sems, share)

    @pl.when(step == 0)
    def _():
        for copy in made:
            copy.start()
        for copy in made:
            copy.wait()

    piece = weights[pl.ds(pl.multiple_of(step * block, block), block), :]
    parts = weights.shape[1] // block

    @pl.when(step < parts)
    def _():
        queries[...] = product(query_source[...], piece).astype(jnp.bfloat16)

    @pl.when(step >= parts)
    def _():
        for source, pair in zip(sources, pairs):
            for start in range(0, source.shape[0], 512):
                rows = slice(start, min(start + 512, source.shape[0]))
                pair[rows, :] = product(source[rows, :], piece).astype(jnp.bfloat16)


def projected(query_source, sources, pieces):
    rows, width = query_source.shape
    block = 256
    parts = width // block
    share = 3 * width // lax.axis_size("dp")
    length = sum(s.shape[0] for s in sources)
    anywhere = pl.BlockSpec(memory_space=pltpu.HBM)
    return pl.pallas_call(
        functools.partial(project_kernel, len(sources), [p[:2] for p in pieces], share),
        grid=(3 * parts,),
        out_shape=[jax.ShapeDtypeStruct((rows, width), jnp.bfloat16)]
        + [jax.ShapeDtypeStruct((s.shape[0], 2 * width), jnp.bfloat16) for s in sources],
        in_specs=[pl.BlockSpec(s.shape, lambda i: (0, 0)) for s in (query_source, *sources)]
        + [anywhere] * len(pieces),
        out_specs=[pl.BlockSpec((rows, block), lambda i: (0, jnp.minimum(i, parts - 1)))]
        + [
            pl.BlockSpec((s.shape[0], block), lambda i: (0, jnp.maximum(i - parts, 0)))
            for s in sources
        ],
        scratch_shapes=[
            pltpu.VMEM((3 * width, width), jnp.bfloat16),
            pltpu.SemaphoreType.DMA((len(pieces),)),
        ],
        compiler_params=pltpu.CompilerParams(vmem_limit_bytes=56 << 20),
        cost_estimate=pl.CostEstimate(
            flops=2 * width * width * (rows + 2 * length),
            bytes_accessed=2 * width * (3 * width + rows + 3 * length),
            transcendentals=0,
        ),
        name="project",
    )(query_source, *sources, *[p[2] for p in pieces])


def attention_kernel(count, tile, q_ref, *refs):
    keys, values, out_ref = refs[:count], refs[count : 2 * count], refs[2 * count]
    rows = q_ref.shape[0]
    heads = LANES // HEAD
    lane = lax.broadcasted_iota(jnp.int32, (tile, LANES), 1) // HEAD
    factor = HEAD ** (-0.5) * math.log2(math.e)
    tiles = [(start, head) for start in range(0, rows, tile) for head in range(heads)]

    def scores_of(start, head):
        picked = jnp.where(lane == head, q_ref[start : start + tile, :], jnp.bfloat16(0))
        return [
            lax.dot_general(picked, k[...], NT, preferred_element_type=jnp.float32) for k in keys
        ]

    def context_of(scores):
        top = functools.reduce(jnp.maximum, [jnp.max(s, axis=1, keepdims=True) for s in scores])
        raised = [jnp.exp2((s - top) * factor) for s in scores]
        totals = sum(jnp.sum(r, axis=1, keepdims=True) for r in raised)
        mixed = sum(
            jnp.dot(r.astype(jnp.bfloat16), v[...], preferred_element_type=jnp.float32)
            for r, v in zip(raised, values)
        )
        return mixed / totals

    pending = scores_of(*tiles[0])
    merged = None
    for index, (start, head) in enumerate(tiles):
        scores = pending
        if index + 1 < len(tiles):
            pending = scores_of(*tiles[index + 1])
        mixed = context_of(scores)
        merged = mixed if head == 0 else jnp.where(lane == head, mixed, merged)
        if head == heads - 1:
            out_ref[start : start + tile, :] = merged.astype(jnp.bfloat16)


def attention(queries, pairs):
    rows, width = queries.shape
    count = len(pairs)
    length = sum(p.shape[0] for p in pairs)
    steps = width // LANES
    spec = pl.BlockSpec((rows, LANES), lambda h: (0, h))
    return pl.pallas_call(
        functools.partial(attention_kernel, count, rows // 2),
        grid=(steps,),
        out_shape=jax.ShapeDtypeStruct((rows, width), jnp.bfloat16),
        in_specs=[spec]
        + [pl.BlockSpec((p.shape[0], LANES), lambda h: (0, h)) for p in pairs]
        + [pl.BlockSpec((p.shape[0], LANES), lambda h: (0, h + steps)) for p in pairs],
        out_specs=spec,
        compiler_params=pltpu.CompilerParams(vmem_limit_bytes=40 << 20),
        cost_estimate=pl.CostEstimate(
            flops=16 * rows * length * width,
            bytes_accessed=4 * (rows + length) * width,
            transcendentals=rows * length * width // HEAD,
        ),
        name="attention",
    )(queries, *pairs, *pairs)


def tail_kernel(
    context, fed_before, fed_own, fed_after, weights,
    gain_conv, gain_final, taps, scale, shift,
    out, w_output, w_widen, w_narrow, stream, conv_in, gated, shifted, activated, sems,
):
    rows, width = out.shape
    total = rows + 2 * HALO
    block = 256
    devices, share = w_output.shape[:2]
    made = [
        pltpu.make_async_copy(weights.at[:, pl.ds(start, ref.shape[1]), :], ref, sems.at[index])
        for index, (start, ref) in enumerate(
            ((0, w_output), (share, w_widen), (3 * share, w_narrow))
        )
    ]
    for copy in made:
        copy.start()

    def rows_of(ref, start):
        each = ref.shape[1]
        return ref[start // each : (start + block) // each].reshape(block, width)

    made[0].wait()
    for start in range(0, width, block):
        columns = slice(start, start + block)
        mixed = product(context[...], rows_of(w_output, start))
        stream[0:HALO, columns] = fed_before[:, columns] + mixed[0:HALO]
        stream[HALO : HALO + rows, columns] = fed_own[:, columns] + mixed[HALO : HALO + rows]
        stream[HALO + rows :, columns] = fed_after[:, columns] + mixed[HALO + rows :]
    conv_in[...] = kernel_norm(stream[...], gain_conv[...]).astype(jnp.bfloat16)

    made[1].wait()
    place = lax.broadcasted_iota(jnp.int32, (total, block), 0)
    here, last = lax.axis_index("seq"), lax.axis_size("seq") - 1
    low = jnp.where(here == 0, HALO, 0)
    high = jnp.where(here == last, HALO + rows, total)
    inside = jnp.logical_and(place >= low, place < high)
    for start in range(0, width, block):
        columns = slice(start, start + block)
        left = product(conv_in[...], rows_of(w_widen, start))
        right = product(conv_in[...], rows_of(w_widen, width + start))
        gate = (left * (0.5 + 0.5 * jnp.tanh(0.5 * right))).astype(jnp.bfloat16)
        gated[:, columns] = jnp.where(inside, gate.astype(jnp.float32), 0.0)

    lead = HALO - KERNEL // 2
    tile = min(128, rows)

    def conv(index, carry):
        columns = pl.ds(pl.multiple_of(index * LANES, LANES), LANES)
        for residue in range(1, 8):
            shifted[residue, 0 : total - 8, :] = gated[residue : residue + total - 8, columns]
        for start in range(0, rows, tile):
            filtered = jnp.zeros((tile, LANES), jnp.float32)
            for tap in range(KERNEL):
                offset = tap + lead
                base = start + offset // 8 * 8
                if offset % 8 == 0:
                    piece = gated[base : base + tile, columns]
                else:
                    piece = shifted[offset % 8, base : base + tile, :]
                filtered = filtered + taps[tap : tap + 1, columns] * piece
            moved = filtered * scale[:, columns] + shift[:, columns]
            activated[start : start + tile, columns] = silu(moved).astype(jnp.bfloat16)
        return carry

    lax.fori_loop(0, width // LANES, conv, 0)

    made[2].wait()
    for start in range(0, width, block):
        columns = slice(start, start + block)
        stream[HALO : HALO + rows, columns] += product(activated[...], rows_of(w_narrow, start))
    out[...] = kernel_norm(stream[HALO : HALO + rows, :], gain_final[...]).astype(jnp.bfloat16)


def tail_of(context, fed_before, fed_own, fed_after, weights, gain_conv, gain_final, taps, scale, shift):
    rows, width = fed_own.shape
    total = rows + 2 * HALO
    devices = weights.shape[0]
    share = width // devices
    whole = pl.BlockSpec(memory_space=pltpu.VMEM)
    return pl.pallas_call(
        tail_kernel,
        out_shape=jax.ShapeDtypeStruct((rows, width), jnp.bfloat16),
        in_specs=[whole] * 4 + [pl.BlockSpec(memory_space=pltpu.HBM)] + [whole] * 5,
        out_specs=whole,
        scratch_shapes=[
            pltpu.VMEM((devices, share, width), jnp.bfloat16),
            pltpu.VMEM((devices, 2 * share, width), jnp.bfloat16),
            pltpu.VMEM((devices, share, width), jnp.bfloat16),
            pltpu.VMEM((total, width), jnp.float32),
            pltpu.VMEM((total, width), jnp.bfloat16),
            pltpu.VMEM((total, width), jnp.float32),
            pltpu.VMEM((8, total, LANES), jnp.float32),
            pltpu.VMEM((rows, width), jnp.bfloat16),
            pltpu.SemaphoreType.DMA((3,)),
        ],
        compiler_params=pltpu.CompilerParams(vmem_limit_bytes=48 << 20),
        cost_estimate=pl.CostEstimate(
            flops=8 * total * width * width + 2 * KERNEL * rows * width,
            bytes_accessed=8 * width * width + 10 * rows * width,
            transcendentals=3 * rows * width,
        ),
        name="tail",
    )(
        context, fed_before, fed_own, fed_after, weights,
        gain_conv[None], gain_final[None], taps, scale[None], shift[None],
    )


def body(
    tokens,
    expand_value,
    expand_scale,
    shrink_value,
    shrink_scale,
    project_value,
    project_scale,
    output_value,
    output_scale,
    widen_value,
    widen_scale,
    narrow_value,
    narrow_scale,
    kernel_taps,
    gain_feed,
    gain_attend,
    gain_conv,
    gain_final,
    batch_scale,
    batch_shift,
):
    count = lax.axis_size("seq")
    rows = tokens.shape[1]
    ring = [(i, (i + 1) % count) for i in range(count)]
    chunks = [tokens[0]]

    def pass_on():
        chunks.append(lax.ppermute(chunks[-1], "seq", ring))

    expand_full = gathered(own_rows_of(expand_value, expand_scale))
    shrink_sets = first_stages(jnp.split(own_rows_of(shrink_value, shrink_scale), 2))
    project_parts = jnp.split(own_rows_of(project_value, project_scale), 2)
    tail_rows = jnp.concatenate(
        [
            own_rows_of(output_value, output_scale),
            own_rows_of(widen_value, widen_scale),
            own_rows_of(narrow_value, narrow_scale),
        ],
        axis=0,
    )
    tail_weights = lax.all_gather(tail_rows, "dp", axis=0)
    pass_on()

    arrays, project_parts, chunks[-1] = barrier(
        [a for own, first in shrink_sets for _, _, a in own + first], project_parts, chunks[-1]
    )
    shrink_sets = refilled(shrink_sets, arrays)
    shrink_held = later_stages(shrink_sets)
    project_sets = first_stages(project_parts)
    pass_on()

    shrink_arrays, arrays, chunks[-1] = barrier(
        [a for _, _, a in shrink_held],
        [a for own, first in project_sets for _, _, a in own + first],
        chunks[-1],
    )
    shrink_held = [(*t[:2], a) for t, a in zip(shrink_held, shrink_arrays)]
    project_sets = refilled(project_sets, arrays)
    shrink_pieces = crossed(shrink_held)
    project_pieces = crossed(later_stages(project_sets))
    while len(chunks) < count:
        pass_on()

    attend_near, after_feed, fed_before = feed(
        chunks[:-1], (1, rows - HALO), gain_feed, gain_attend, expand_full, shrink_pieces
    )
    attend_far, _, fed_after = feed(
        chunks[-1:], (0, 0), gain_feed, gain_attend, expand_full, shrink_pieces
    )
    query_source = jnp.concatenate(
        [attend_near[2 * rows - HALO : 2 * rows], attend_near[:rows], attend_far[:HALO]], axis=0
    )
    queries, *pairs = projected(query_source, [attend_near, attend_far], project_pieces)
    context = attention(queries, pairs)
    return tail_of(
        context, fed_before, after_feed, fed_after, tail_weights,
        gain_conv, gain_final, kernel_taps, batch_scale, batch_shift,
    )[None]


def solution(mesh):
    weights = (P(None, "dp"),) * 12
    return jax.shard_map(
        body,
        mesh=mesh,
        in_specs=(P("dp", "seq", None),) + weights + (P(),) * 7,
        out_specs=P("dp", "seq", None),
        check_vma=False,
    )
```

```python
import functools
import math

import jax
import jax.numpy as jnp
from jax import lax
from jax.experimental import pallas as pl
from jax.experimental.layout import Layout, with_layout_constraint
from jax.experimental.pallas import tpu as pltpu
from jax.sharding import PartitionSpec as P

HEAD = 64
KERNEL = 31
LANES = 128
HALO = 16
VMEM = 60 << 20
NT = (((1,), (1,)), ((), ()))


def dequant(value_grid, scale_grid):
    stretched = jnp.repeat(scale_grid.astype(jnp.float32), 128, axis=0)
    return (value_grid.astype(jnp.float32) * stretched).astype(jnp.bfloat16)


def own_rows_of(value_grid, scale_grid):
    return jnp.transpose(dequant(value_grid, scale_grid))


def gathered(rows):
    return lax.all_gather(rows, "dp", axis=0, tiled=True)


def product(left, right):
    return lax.dot_general(left, right, NT, preferred_element_type=jnp.float32)


def layer_norm(values, gain_row):
    average = jnp.mean(values, axis=-1, keepdims=True)
    centred = values - average
    energy = jnp.mean(centred * centred, axis=-1, keepdims=True)
    return centred * lax.rsqrt(energy + 1e-05) * gain_row


def partners(size, bit):
    return [(i, i ^ bit) for i in range(size)]


def send(array, bit):
    return lax.ppermute(array, "dp", partners(lax.axis_size("dp"), bit))


def far_bits():
    return [1 << b for b in range(1, lax.axis_size("dp").bit_length() - 1)]


def stage(held, bit):
    return held + [(far ^ bit, number, send(a, bit)) for far, number, a in held]


def first_stages(parts):
    bits = far_bits()
    return [
        ([(0, number, part)], [(bit, number, send(part, bit)) for bit in bits])
        for number, part in enumerate(parts)
    ]


def later_stages(sets):
    bits = far_bits()
    result = []
    for own, first in sets:
        number = own[0][1]
        order = bits if number % 2 == 0 else bits[::-1]
        by_bit = dict(zip(bits, first))
        held = list(own)
        for bit in order:
            held += [by_bit[bit]] + [(far ^ bit, n, send(a, bit)) for far, n, a in held[1:]]
        result += held
    return result


def crossed(held):
    return stage(held, 1)


def refilled(sets, arrays):
    arrays = list(arrays)
    return [
        tuple([(far, n, arrays.pop(0)) for far, n, _ in group] for group in pair) for pair in sets
    ]


def barrier(*trees):
    return lax.optimization_barrier(trees)


def half_of(share):
    return -(-share // 32) * 16


def halved(rows):
    return [rows[: half_of(rows.shape[0])], rows[half_of(rows.shape[0]) :]]


def copies(pieces, refs, target, sems, share):
    own = lax.axis_index("dp")
    made = []
    for (far, number), ref in zip(pieces, refs):
        owner = own ^ far
        start = pl.multiple_of(owner * share + number * half_of(share), 16)
        rows = target.at[pl.ds(start, ref.shape[0]), :]
        made.append(pltpu.make_async_copy(ref, rows, sems.at[owner, number]))
    return made


def wait_rows(target, sems, share, owners):
    half = half_of(share)
    for owner in owners:
        for number in range(2):
            start = owner * share + number * half
            rows = target.at[start : start + (share - half if number else half), :]
            pltpu.make_async_copy(rows, rows, sems.at[owner, number]).wait()


def kernel_norm(values, gain_row):
    scale = 1.0 / values.shape[1]
    average = jnp.sum(values, axis=1, keepdims=True) * scale
    centred = values - average
    energy = jnp.sum(centred * centred, axis=1, keepdims=True) * scale
    return centred * lax.rsqrt(energy + 1e-05) * gain_row


def silu(v):
    half = 0.5 * v
    return half + half * jnp.tanh(half)


def feed_kernel(chunks, pieces, share, edge, keep, *refs):
    refs = list(refs)
    tokens = [refs.pop(0) for _ in range(chunks)]
    gain_feed, gain_attend, expand = refs.pop(0), refs.pop(0), refs.pop(0)
    shrink_refs = [refs.pop(0) for _ in pieces]
    attend_in, fed_edge = refs.pop(0), refs.pop(0)
    fed = refs.pop(0) if keep else None
    held, expand_all, shrink_all, feed_in, hidden, total = refs[:6]
    token_sems, expand_sems, shrink_sems = refs[6:]
    step = pl.program_id(0)
    units, width = expand_all.shape
    block = 256

    token_copies = [
        pltpu.make_async_copy(t, held.at[i], token_sems.at[i]) for i, t in enumerate(tokens)
    ]
    expand_copies = [
        pltpu.make_async_copy(
            expand.at[pl.ds(n * block, block), :],
            expand_all.at[pl.ds(n * block, block), :],
            expand_sems.at[n],
        )
        for n in range(units // block)
    ]
    shrink_copies = copies(pieces, shrink_refs, shrink_all, shrink_sems, share)

    @pl.when(step == 0)
    def _():
        for copy in token_copies[:1] + expand_copies + shrink_copies + token_copies[1:]:
            copy.start()

    for i in range(chunks):
        @pl.when(step == i)
        def _(i=i):
            token_copies[i].wait()

    feed_in[...] = kernel_norm(held[step].astype(jnp.float32), gain_feed[...]).astype(jnp.bfloat16)

    @pl.when(step == 0)
    def _():
        for copy in expand_copies:
            copy.wait()

    for n in range(units // block):
        piece = slice(n * block, (n + 1) * block)
        hidden[:, piece] = silu(product(feed_in[...], expand_all[piece, :])).astype(jnp.bfloat16)

    @pl.when(step == 0)
    def _():
        wait_rows(shrink_all, shrink_sems, share, range(width // share))

    for n in range(width // block):
        piece = slice(n * block, (n + 1) * block)
        total[:, piece] = held[step, :, piece].astype(jnp.float32) + 0.5 * product(
            hidden[...], shrink_all[piece, :]
        )
    attend_in[...] = kernel_norm(total[...], gain_attend[...]).astype(jnp.bfloat16)

    if fed is not None:

        @pl.when(step == 0)
        def _():
            fed[...] = total[...]

    @pl.when(step == edge[0])
    def _():
        fed_edge[...] = total[edge[1] : edge[1] + HALO, :]


def feed(chunks, edge, keep, gain_feed, gain_attend, expand_full, shrink_pieces):
    rows, width = chunks[0].shape
    units = expand_full.shape[0]
    count = len(chunks)
    anywhere = pl.BlockSpec(memory_space=pltpu.HBM)
    row = pl.BlockSpec((1, width), lambda i: (0, 0))
    share = width // lax.axis_size("dp")
    return pl.pallas_call(
        functools.partial(feed_kernel, count, [p[:2] for p in shrink_pieces], share, edge, keep),
        grid=(count,),
        out_shape=[
            jax.ShapeDtypeStruct((count * rows, width), jnp.bfloat16),
            jax.ShapeDtypeStruct((HALO, width), jnp.float32),
        ]
        + [jax.ShapeDtypeStruct((rows, width), jnp.float32)] * keep,
        in_specs=[anywhere] * count + [row, row, anywhere] + [anywhere] * len(shrink_pieces),
        out_specs=[
            pl.BlockSpec((rows, width), lambda i: (i, 0)),
            pl.BlockSpec((HALO, width), lambda i: (0, 0)),
        ]
        + [pl.BlockSpec((rows, width), lambda i: (0, 0))] * keep,
        scratch_shapes=[
            pltpu.VMEM((count, rows, width), jnp.bfloat16),
            pltpu.VMEM((units, width), jnp.bfloat16),
            pltpu.VMEM((width, units), jnp.bfloat16),
            pltpu.VMEM((rows, width), jnp.bfloat16),
            pltpu.VMEM((rows, units), jnp.bfloat16),
            pltpu.VMEM((rows, width), jnp.float32),
            pltpu.SemaphoreType.DMA((count,)),
            pltpu.SemaphoreType.DMA((units // 256,)),
            pltpu.SemaphoreType.DMA((len(shrink_pieces) // 2, 2)),
        ],
        compiler_params=pltpu.CompilerParams(vmem_limit_bytes=VMEM),
        cost_estimate=pl.CostEstimate(
            flops=4 * count * rows * width * units,
            bytes_accessed=4 * units * width + 4 * count * rows * width,
            transcendentals=count * rows * units,
        ),
        name="feed",
    )(
        *chunks, gain_feed[None], gain_attend[None], expand_full, *[p[2] for p in shrink_pieces]
    )


def attend_kernel(pieces, share, *refs):
    near, far = refs[:2]
    weight_refs = refs[2 : 2 + len(pieces)]
    out_ref, inputs, query_rows, weights, queries, keys, values, sems, row_sems = refs[
        2 + len(pieces) :
    ]
    step, steps = pl.program_id(0), pl.num_programs(0)
    length, width = inputs.shape
    rows = query_rows.shape[0] - 2 * HALO
    pairs = width // LANES
    made = copies(pieces, weight_refs, weights, sems, share)
    row_copies = [
        pltpu.make_async_copy(source, target, row_sems.at[index])
        for index, (source, target) in enumerate(
            (
                (near.at[0:rows, :], query_rows.at[HALO : HALO + rows, :]),
                (near.at[2 * rows - HALO : 2 * rows, :], query_rows.at[0:HALO, :]),
                (far.at[0:HALO, :], query_rows.at[HALO + rows :, :]),
                (near, inputs.at[0 : length - rows, :]),
                (far, inputs.at[length - rows :, :]),
            )
        )
    ]
    soon = sorted({(part * width + pair * LANES) // share for part in range(3) for pair in (0, 1)})

    def project_queries(pair, slot):
        picked = weights[pl.ds(pl.multiple_of(pair * LANES, LANES), LANES), :]
        queries[slot] = product(query_rows[...], picked).astype(jnp.bfloat16)

    def project_pair(pair, slot, start, stop):
        first = pl.ds(pl.multiple_of(width + pair * LANES, LANES), LANES)
        second = pl.ds(pl.multiple_of(2 * width + pair * LANES, LANES), LANES)
        both = jnp.concatenate([weights[first, :], weights[second, :]], axis=0)
        made_rows = product(inputs[start:stop, :], both).astype(jnp.bfloat16)
        keys[slot, start:stop, :] = made_rows[:, :LANES]
        values[slot, start:stop, :] = made_rows[:, LANES:]

    @pl.when(step == 0)
    def _():
        for copy in row_copies + made:
            copy.start()
        for copy in row_copies:
            copy.wait()
        wait_rows(weights, sems, share, soon)
        project_queries(0, 0)
        for start in range(0, length, rows):
            project_pair(0, 0, start, start + rows)

    @pl.when(step == 1)
    def _():
        rest = [owner for owner in range(3 * width // share) if owner not in soon]
        wait_rows(weights, sems, share, rest)

    slot = lax.rem(step, 2)
    heads = LANES // HEAD
    tile = query_rows.shape[0] // 2
    lane = lax.broadcasted_iota(jnp.int32, (tile, LANES), 1) // HEAD
    factor = HEAD ** (-0.5) * math.log2(math.e)
    tiles = [(start, head) for start in (0, tile) for head in range(heads)]
    blocks = [slice(start, start + rows) for start in range(0, length, rows)]

    def scores_of(start, head):
        picked = jnp.where(lane == head, queries[slot, start : start + tile, :], jnp.bfloat16(0))
        return [product(picked, keys[slot, block, :]) for block in blocks]

    def context_of(scores):
        top = functools.reduce(jnp.maximum, [jnp.max(s, axis=1, keepdims=True) for s in scores])
        raised = [jnp.exp2((s - top) * factor) for s in scores]
        totals = sum(jnp.sum(r, axis=1, keepdims=True) for r in raised)
        mixed = sum(
            jnp.dot(
                r.astype(jnp.bfloat16),
                values[slot, block, :],
                preferred_element_type=jnp.float32,
            )
            for r, block in zip(raised, blocks)
        )
        return mixed / totals

    def attend(project):
        pending = scores_of(*tiles[0])
        merged = None
        for index, (start, head) in enumerate(tiles):
            scores = pending
            if index + 1 < len(tiles):
                pending = scores_of(*tiles[index + 1])
            if project:
                if index == 0:
                    project_queries(step + 1, 1 - slot)
                for block in blocks[index :: len(tiles)]:
                    project_pair(step + 1, 1 - slot, block.start, block.stop)
            mixed = context_of(scores)
            merged = mixed if head == 0 else jnp.where(lane == head, mixed, merged)
            if head == heads - 1:
                out_ref[start : start + tile, :] = merged.astype(jnp.bfloat16)

    @pl.when(step < steps - 1)
    def _():
        attend(True)

    @pl.when(step == steps - 1)
    def _():
        attend(False)


def attention(near, far, pieces):
    rows, width = far.shape
    total = rows + 2 * HALO
    length = near.shape[0] + rows
    share = 3 * width // lax.axis_size("dp")
    anywhere = pl.BlockSpec(memory_space=pltpu.HBM)
    return pl.pallas_call(
        functools.partial(attend_kernel, [p[:2] for p in pieces], share),
        grid=(width // LANES,),
        out_shape=jax.ShapeDtypeStruct((total, width), jnp.bfloat16),
        in_specs=[anywhere] * (2 + len(pieces)),
        out_specs=pl.BlockSpec((total, LANES), lambda h: (0, h)),
        scratch_shapes=[
            pltpu.VMEM((length, width), jnp.bfloat16),
            pltpu.VMEM((total, width), jnp.bfloat16),
            pltpu.VMEM((3 * width, width), jnp.bfloat16),
            pltpu.VMEM((2, total, LANES), jnp.bfloat16),
            pltpu.VMEM((2, length, LANES), jnp.bfloat16),
            pltpu.VMEM((2, length, LANES), jnp.bfloat16),
            pltpu.SemaphoreType.DMA((len(pieces) // 2, 2)),
            pltpu.SemaphoreType.DMA((5,)),
        ],
        compiler_params=pltpu.CompilerParams(vmem_limit_bytes=VMEM),
        cost_estimate=pl.CostEstimate(
            flops=16 * total * length * width + 2 * width * width * (total + 2 * length),
            bytes_accessed=2 * width * (3 * width + 3 * total + length),
            transcendentals=total * length * width // HEAD,
        ),
        name="attention",
    )(near, far, *[p[2] for p in pieces])


def tail_kernel(
    context, fed_before, fed_own, fed_after, weights,
    gain_conv, gain_final, taps, scale, shift,
    out, w_output, w_widen, w_narrow, stream, conv_in, gated, shifted, activated, sems,
):
    rows, width = out.shape
    total = rows + 2 * HALO
    block = 256
    devices, share = w_output.shape[:2]
    made = [
        pltpu.make_async_copy(weights.at[:, pl.ds(start, ref.shape[1]), :], ref, sems.at[index])
        for index, (start, ref) in enumerate(
            ((0, w_output), (share, w_widen), (3 * share, w_narrow))
        )
    ]
    for copy in made:
        copy.start()

    def rows_of(ref, start):
        each = ref.shape[1]
        return ref[start // each : (start + block) // each].reshape(block, width)

    made[0].wait()
    for start in range(0, width, block):
        columns = slice(start, start + block)
        mixed = product(context[...], rows_of(w_output, start))
        stream[0:HALO, columns] = fed_before[:, columns] + mixed[0:HALO]
        stream[HALO : HALO + rows, columns] = fed_own[:, columns] + mixed[HALO : HALO + rows]
        stream[HALO + rows :, columns] = fed_after[:, columns] + mixed[HALO + rows :]
    conv_in[...] = kernel_norm(stream[...], gain_conv[...]).astype(jnp.bfloat16)

    made[1].wait()
    place = lax.broadcasted_iota(jnp.int32, (total, block), 0)
    here, last = lax.axis_index("seq"), lax.axis_size("seq") - 1
    low = jnp.where(here == 0, HALO, 0)
    high = jnp.where(here == last, HALO + rows, total)
    inside = jnp.logical_and(place >= low, place < high)
    for start in range(0, width, block):
        columns = slice(start, start + block)
        left = product(conv_in[...], rows_of(w_widen, start))
        right = product(conv_in[...], rows_of(w_widen, width + start))
        gate = (left * (0.5 + 0.5 * jnp.tanh(0.5 * right))).astype(jnp.bfloat16)
        gated[:, columns] = jnp.where(inside, gate.astype(jnp.float32), 0.0)

    lead = HALO - KERNEL // 2
    tile = min(128, rows)

    def conv(index, carry):
        columns = pl.ds(pl.multiple_of(index * LANES, LANES), LANES)
        for residue in range(1, 8):
            shifted[residue, 0 : total - 8, :] = gated[residue : residue + total - 8, columns]
        for start in range(0, rows, tile):
            filtered = jnp.zeros((tile, LANES), jnp.float32)
            for tap in range(KERNEL):
                offset = tap + lead
                base = start + offset // 8 * 8
                if offset % 8 == 0:
                    piece = gated[base : base + tile, columns]
                else:
                    piece = shifted[offset % 8, base : base + tile, :]
                filtered = filtered + taps[tap : tap + 1, columns] * piece
            moved = filtered * scale[:, columns] + shift[:, columns]
            activated[start : start + tile, columns] = silu(moved).astype(jnp.bfloat16)
        return carry

    lax.fori_loop(0, width // LANES, conv, 0)

    made[2].wait()
    for start in range(0, width, block):
        columns = slice(start, start + block)
        stream[HALO : HALO + rows, columns] += product(activated[...], rows_of(w_narrow, start))
    out[...] = kernel_norm(stream[HALO : HALO + rows, :], gain_final[...]).astype(jnp.bfloat16)


def tail_of(context, fed_before, fed_own, fed_after, weights, gain_conv, gain_final, taps, scale, shift):
    rows, width = fed_own.shape
    total = rows + 2 * HALO
    devices = weights.shape[0]
    share = width // devices
    whole = pl.BlockSpec(memory_space=pltpu.VMEM)
    return pl.pallas_call(
        tail_kernel,
        out_shape=jax.ShapeDtypeStruct((rows, width), jnp.bfloat16),
        in_specs=[whole] * 4 + [pl.BlockSpec(memory_space=pltpu.HBM)] + [whole] * 5,
        out_specs=whole,
        scratch_shapes=[
            pltpu.VMEM((devices, share, width), jnp.bfloat16),
            pltpu.VMEM((devices, 2 * share, width), jnp.bfloat16),
            pltpu.VMEM((devices, share, width), jnp.bfloat16),
            pltpu.VMEM((total, width), jnp.float32),
            pltpu.VMEM((total, width), jnp.bfloat16),
            pltpu.VMEM((total, width), jnp.float32),
            pltpu.VMEM((8, total, LANES), jnp.float32),
            pltpu.VMEM((rows, width), jnp.bfloat16),
            pltpu.SemaphoreType.DMA((3,)),
        ],
        compiler_params=pltpu.CompilerParams(vmem_limit_bytes=VMEM),
        cost_estimate=pl.CostEstimate(
            flops=8 * total * width * width + 2 * KERNEL * rows * width,
            bytes_accessed=8 * width * width + 10 * rows * width,
            transcendentals=3 * rows * width,
        ),
        name="tail",
    )(
        context, fed_before, fed_own, fed_after, weights,
        gain_conv[None], gain_final[None], taps, scale[None], shift[None],
    )


def body(
    tokens,
    expand_value,
    expand_scale,
    shrink_value,
    shrink_scale,
    project_value,
    project_scale,
    output_value,
    output_scale,
    widen_value,
    widen_scale,
    narrow_value,
    narrow_scale,
    kernel_taps,
    gain_feed,
    gain_attend,
    gain_conv,
    gain_final,
    batch_scale,
    batch_shift,
):
    count = lax.axis_size("seq")
    rows = tokens.shape[1]
    ring = [(i, (i + 1) % count) for i in range(count)]
    chunks = [tokens[0]]

    def pass_on():
        chunks.append(lax.ppermute(chunks[-1], "seq", ring))

    expand_full = gathered(own_rows_of(expand_value, expand_scale))
    shrink_sets = first_stages(halved(own_rows_of(shrink_value, shrink_scale)))
    project_parts = halved(own_rows_of(project_value, project_scale))
    tail_rows = jnp.concatenate(
        [
            own_rows_of(output_value, output_scale),
            own_rows_of(widen_value, widen_scale),
            own_rows_of(narrow_value, narrow_scale),
        ],
        axis=0,
    )
    tail_rows = with_layout_constraint(tail_rows, Layout((0, 1)))
    tail_weights = with_layout_constraint(
        lax.all_gather(tail_rows, "dp", axis=0), Layout((0, 1, 2))
    )
    pass_on()

    arrays, chunks[-1] = barrier([a for own, first in shrink_sets for _, _, a in own + first], chunks[-1])
    shrink_sets = refilled(shrink_sets, arrays)
    shrink_held = later_stages(shrink_sets)
    pass_on()

    arrays, project_parts, chunks[-1] = barrier(
        [a for _, _, a in shrink_held], project_parts, chunks[-1]
    )
    shrink_held = [(*t[:2], a) for t, a in zip(shrink_held, arrays)]
    shrink_pieces = crossed(shrink_held)
    project_sets = first_stages(project_parts)
    while len(chunks) < count:
        pass_on()

    attend_near, fed_before, after_feed = feed(
        chunks[:-1], (1, rows - HALO), True, gain_feed, gain_attend, expand_full, shrink_pieces
    )
    attend_near, arrays = barrier(
        attend_near, [a for own, first in project_sets for _, _, a in own + first]
    )
    project_held = later_stages(refilled(project_sets, arrays))
    attend_far, fed_after = feed(
        chunks[-1:], (0, 0), False, gain_feed, gain_attend, expand_full, shrink_pieces
    )
    attend_far, arrays = barrier(attend_far, [a for _, _, a in project_held])
    project_pieces = crossed([(*t[:2], a) for t, a in zip(project_held, arrays)])
    context = attention(attend_near, attend_far, project_pieces)
    return tail_of(
        context, fed_before, after_feed, fed_after, tail_weights,
        gain_conv, gain_final, kernel_taps, batch_scale, batch_shift,
    )[None]


def solution(mesh):
    weights = (P(None, "dp"),) * 12
    return jax.shard_map(
        body,
        mesh=mesh,
        in_specs=(P("dp", "seq", None),) + weights + (P(),) * 7,
        out_specs=P("dp", "seq", None),
        check_vma=False,
    )
```

```python
import functools

import jax
import jax.numpy as jnp
from jax import lax
from jax.experimental import pallas as pl
from jax.experimental.layout import Layout, with_layout_constraint
from jax.experimental.pallas import tpu as pltpu
from jax.sharding import PartitionSpec as P

HEAD = 64
KERNEL = 31
LANES = 128
HALO = 16
VMEM = 60 << 20
NT = (((1,), (1,)), ((), ()))


def dequant(value_grid, scale_grid):
    stretched = jnp.repeat(scale_grid.astype(jnp.float32), 128, axis=0)
    return (value_grid.astype(jnp.float32) * stretched).astype(jnp.bfloat16)


def own_rows_of(value_grid, scale_grid):
    return jnp.transpose(dequant(value_grid, scale_grid))


def gathered(rows):
    return lax.all_gather(rows, "dp", axis=0, tiled=True)


def product(left, right):
    return lax.dot_general(left, right, NT, preferred_element_type=jnp.float32)


def layer_norm(values, gain_row):
    average = jnp.mean(values, axis=-1, keepdims=True)
    centred = values - average
    energy = jnp.mean(centred * centred, axis=-1, keepdims=True)
    return centred * lax.rsqrt(energy + 1e-05) * gain_row


def partners(size, bit):
    return [(i, i ^ bit) for i in range(size)]


def send(array, bit):
    return lax.ppermute(array, "dp", partners(lax.axis_size("dp"), bit))


def far_bits():
    return [1 << b for b in range(1, lax.axis_size("dp").bit_length() - 1)]


def stage(held, bit):
    return held + [(far ^ bit, number, send(a, bit)) for far, number, a in held]


def first_stages(parts):
    bits = far_bits()
    return [
        ([(0, number, part)], [(bit, number, send(part, bit)) for bit in bits])
        for number, part in enumerate(parts)
    ]


def later_stages(sets):
    bits = far_bits()
    result = []
    for own, first in sets:
        number = own[0][1]
        order = bits if number % 2 == 0 else bits[::-1]
        by_bit = dict(zip(bits, first))
        held = list(own)
        for bit in order:
            held += [by_bit[bit]] + [(far ^ bit, n, send(a, bit)) for far, n, a in held[1:]]
        result += held
    return result


def first_sends(array):
    return [(0, None, array)] + [(bit, None, send(array, bit)) for bit in far_bits()]


def relays(first):
    bits = far_bits()
    arrived = {far: array for far, _, array in first}
    result = []
    for number, order in ((0, bits), (1, bits[::-1])):
        half = arrived[0].shape[0] // 2
        cut = {bit: arrived[bit][number * half : (number + 1) * half] for bit in bits}
        held = [(order[0], cut[order[0]])]
        for bit in order[1:]:
            sent = [(far ^ bit, send(a, bit)) for far, a in held]
            held += [(bit, cut[bit])] + sent
            result += [(far, number, a) for far, a in sent]
    return result


def flat(sets):
    return [a for own, first in sets for _, _, a in own + first]


def split_late(held):
    near = [0, *far_bits()]
    return [t for t in held if t[0] in near], [t for t in held if t[0] not in near]


def by_part(pieces):
    return [
        sorted([(far, a) for far, n, a in pieces if n == part], key=lambda t: t[0])
        for part in (0, 1)
    ]


def replaced(held, arrays):
    return [(far, number, a) for (far, number, _), a in zip(held, arrays)]


def held_back(arrays, held):
    arrays, others = barrier(arrays, [a for _, _, a in held])
    return arrays, replaced(held, others)


def crossed(held):
    return stage(held, 1)


def refilled(sets, arrays):
    arrays = list(arrays)
    return [
        tuple([(far, n, arrays.pop(0)) for far, n, _ in group] for group in pair) for pair in sets
    ]


def barrier(*trees):
    return lax.optimization_barrier(trees)


def copies(fars, refs, target, sems):
    own = lax.axis_index("dp")
    made = []
    for far, ref in zip(fars, refs):
        owner = own ^ far
        start = pl.multiple_of(owner * ref.shape[0], 16)
        rows = target.at[pl.ds(start, ref.shape[0]), :]
        made.append(pltpu.make_async_copy(ref, rows, sems.at[owner]))
    return made


def wait_rows(target, sems, share, owners):
    for owner in owners:
        rows = target.at[owner * share : (owner + 1) * share, :]
        pltpu.make_async_copy(rows, rows, sems.at[owner]).wait()


def half_copies(marks, refs, target, sems, share):
    own = lax.axis_index("dp")
    made = []
    for (far, number), ref in zip(marks, refs):
        owner = own ^ far
        start = pl.multiple_of(owner * share + (number or 0) * (share // 2), 16)
        rows = target.at[pl.ds(start, ref.shape[0]), :]
        made.append(pltpu.make_async_copy(ref, rows, sems.at[owner]))
    return made


def kernel_norm(values, gain_row):
    scale = 1.0 / values.shape[1]
    average = jnp.sum(values, axis=1, keepdims=True) * scale
    centred = values - average
    energy = jnp.sum(centred * centred, axis=1, keepdims=True) * scale
    return centred * lax.rsqrt(energy + 1e-05) * gain_row


def silu(v):
    half = 0.5 * v
    return half + half * jnp.tanh(half)


def feed_kernel(chunks, fars, edges, keep, *refs):
    refs = list(refs)
    tokens = [refs.pop(0) for _ in range(chunks)]
    gain_feed, gain_attend = refs.pop(0), refs.pop(0)
    expand_refs = [refs.pop(0) for _ in fars]
    shrink_refs = [refs.pop(0) for _ in fars]
    attend_in = refs.pop(0)
    fed_edges = [refs.pop(0) for _ in edges]
    fed = refs.pop(0) if keep else None
    held, expand_all, shrink_all, feed_in, hidden, total, token_sems, expand_sems, shrink_sems = refs
    step = pl.program_id(0)
    units, width = expand_all.shape
    block = 256
    token_copies = [
        pltpu.make_async_copy(t, held.at[i], token_sems.at[i]) for i, t in enumerate(tokens)
    ]

    @pl.when(step == 0)
    def _():
        token_copies[0].start()
        for copy in copies(fars, expand_refs, expand_all, expand_sems):
            copy.start()
        for copy in copies(fars, shrink_refs, shrink_all, shrink_sems):
            copy.start()
        for copy in token_copies[1:]:
            copy.start()

    for i in range(chunks):
        @pl.when(step == i)
        def _(i=i):
            token_copies[i].wait()

    own = held[step].astype(jnp.float32)
    feed_in[...] = kernel_norm(own, gain_feed[...]).astype(jnp.bfloat16)

    @pl.when(step == 0)
    def _():
        wait_rows(expand_all, expand_sems, units // len(fars), range(len(fars)))

    for n in range(units // block):
        piece = slice(n * block, (n + 1) * block)
        hidden[:, piece] = silu(product(feed_in[...], expand_all[piece, :])).astype(jnp.bfloat16)

    @pl.when(step == 0)
    def _():
        wait_rows(shrink_all, shrink_sems, width // len(fars), range(len(fars)))

    for n in range(width // block):
        piece = slice(n * block, (n + 1) * block)
        total[:, piece] = held[step, :, piece].astype(jnp.float32) + 0.5 * product(
            hidden[...], shrink_all[piece, :]
        )
    attend_in[...] = kernel_norm(total[...], gain_attend[...]).astype(jnp.bfloat16)
    if fed is not None:

        @pl.when(step == 0)
        def _():
            fed[...] = total[...]

    for (place, start), fed_edge in zip(edges, fed_edges):

        @pl.when(step == place)
        def _(start=start, fed_edge=fed_edge):
            fed_edge[...] = total[start : start + HALO, :]


def feed(chunks, edges, keep, gain_feed, gain_attend, expand_pieces, shrink_pieces):
    rows, width = chunks[0].shape
    count, devices = len(chunks), len(expand_pieces)
    units = devices * expand_pieces[0][1].shape[0]
    fars = [far for far, _ in expand_pieces]
    anywhere = pl.BlockSpec(memory_space=pltpu.HBM)
    row = pl.BlockSpec((1, width), lambda i: (0, 0))
    return pl.pallas_call(
        functools.partial(feed_kernel, count, fars, edges, keep),
        grid=(count,),
        out_shape=[
            jax.ShapeDtypeStruct((count * rows, width), jnp.bfloat16),
        ]
        + [jax.ShapeDtypeStruct((HALO, width), jnp.float32)] * len(edges)
        + [jax.ShapeDtypeStruct((rows, width), jnp.float32)] * keep,
        in_specs=[anywhere] * count + [row, row] + [anywhere] * (2 * devices),
        out_specs=[
            pl.BlockSpec((rows, width), lambda i: (i, 0)),
        ]
        + [pl.BlockSpec((HALO, width), lambda i: (0, 0))] * len(edges)
        + [pl.BlockSpec((rows, width), lambda i: (0, 0))] * keep,
        scratch_shapes=[
            pltpu.VMEM((count, rows, width), jnp.bfloat16),
            pltpu.VMEM((units, width), jnp.bfloat16),
            pltpu.VMEM((width, units), jnp.bfloat16),
            pltpu.VMEM((rows, width), jnp.bfloat16),
            pltpu.VMEM((rows, units), jnp.bfloat16),
            pltpu.VMEM((rows, width), jnp.float32),
            pltpu.SemaphoreType.DMA((count,)),
            pltpu.SemaphoreType.DMA((devices,)),
            pltpu.SemaphoreType.DMA((devices,)),
        ],
        compiler_params=pltpu.CompilerParams(vmem_limit_bytes=VMEM),
        cost_estimate=pl.CostEstimate(
            flops=4 * count * rows * width * units,
            bytes_accessed=4 * units * width + 4 * count * rows * width,
            transcendentals=count * rows * units,
        ),
        name="feed",
    )(
        *chunks, gain_feed[None], gain_attend[None],
        *[a for _, a in expand_pieces], *[a for _, a in shrink_pieces],
    )


def attend_kernel(marks, share, *refs):
    near, far = refs[:2]
    weight_refs = refs[2 : 2 + len(marks)]
    out_ref, inputs, query_rows, weights, queries, keys, values, sems, row_sems = refs[
        2 + len(marks) :
    ]
    step, steps = pl.program_id(0), pl.num_programs(0)
    length, width = inputs.shape
    rows = query_rows.shape[0] - 2 * HALO
    pairs = width // LANES
    made = half_copies(marks, weight_refs, weights, sems, share)
    soon = sorted({(part * width + pair * LANES) // share for part in range(3) for pair in (0, 1)})
    row_copies = [
        pltpu.make_async_copy(source, target, row_sems.at[index])
        for index, (source, target) in enumerate(
            (
                (near.at[0:rows, :], query_rows.at[HALO : HALO + rows, :]),
                (near.at[2 * rows - HALO : 2 * rows, :], query_rows.at[0:HALO, :]),
                (near.at[2 * rows : 2 * rows + HALO, :], query_rows.at[HALO + rows :, :]),
                (near, inputs.at[0 : near.shape[0], :]),
                (far, inputs.at[near.shape[0] :, :]),
            )
        )
    ]
    def project_queries(pair, slot):
        picked = weights[pl.ds(pl.multiple_of(pair * LANES, LANES), LANES), :]
        scaled = product(query_rows[...], picked).astype(jnp.bfloat16) * HEAD ** (-0.5)
        queries[slot] = scaled.astype(jnp.bfloat16)

    def project_pair(pair, slot, start, stop):
        first = pl.ds(pl.multiple_of(width + pair * LANES, LANES), LANES)
        second = pl.ds(pl.multiple_of(2 * width + pair * LANES, LANES), LANES)
        both = jnp.concatenate([weights[first, :], weights[second, :]], axis=0)
        made_rows = product(inputs[start:stop, :], both).astype(jnp.bfloat16)
        keys[slot, start:stop, :] = made_rows[:, :LANES]
        values[slot, start:stop, :] = made_rows[:, LANES:]

    @pl.when(step == 0)
    def _():
        for copy in row_copies + made:
            copy.start()
        for copy in row_copies:
            copy.wait()
        wait_rows(weights, sems, share, soon)
        project_queries(0, 0)
        for start in range(0, length, rows):
            project_pair(0, 0, start, start + rows)

    @pl.when(step == 1)
    def _():
        rest = [owner for owner in range(3 * width // share) if owner not in soon]
        wait_rows(weights, sems, share, rest)

    slot = lax.rem(step, 2)
    heads = LANES // HEAD
    tile = query_rows.shape[0] // 2
    lane = lax.broadcasted_iota(jnp.int32, (tile, LANES), 1) // HEAD
    tiles = [(start, head) for start in (0, tile) for head in range(heads)]
    blocks = [slice(start, start + rows) for start in range(0, length, rows)]

    def scores_of(start, head):
        picked = jnp.where(lane == head, queries[slot, start : start + tile, :], jnp.bfloat16(0))
        return [product(picked, keys[slot, block, :]) for block in blocks]

    def context_of(scores):
        top = functools.reduce(jnp.maximum, [jnp.max(s, axis=1, keepdims=True) for s in scores])
        raised = [jnp.exp(s - top) for s in scores]
        totals = sum(jnp.sum(r, axis=1, keepdims=True) for r in raised)
        mixed = sum(
            jnp.dot(
                r.astype(jnp.bfloat16),
                values[slot, block, :],
                preferred_element_type=jnp.float32,
            )
            for r, block in zip(raised, blocks)
        )
        return mixed / totals

    def attend(project):
        pending = scores_of(*tiles[0])
        merged = None
        for index, (start, head) in enumerate(tiles):
            scores = pending
            if index + 1 < len(tiles):
                pending = scores_of(*tiles[index + 1])
            if project:
                if index == 0:
                    project_queries(step + 1, 1 - slot)
                for block in blocks[index :: len(tiles)]:
                    project_pair(step + 1, 1 - slot, block.start, block.stop)
            mixed = context_of(scores)
            merged = mixed if head == 0 else jnp.where(lane == head, mixed, merged)
            if head == heads - 1:
                out_ref[start : start + tile, :] = merged.astype(jnp.bfloat16)

    @pl.when(step < steps - 1)
    def _():
        attend(True)

    @pl.when(step == steps - 1)
    def _():
        attend(False)


def attention(rows, near, far, pieces):
    width = far.shape[1]
    total = rows + 2 * HALO
    length = near.shape[0] + far.shape[0]
    anywhere = pl.BlockSpec(memory_space=pltpu.HBM)
    marks = [piece[:2] for piece in pieces]
    share = 3 * width // lax.axis_size("dp")
    return pl.pallas_call(
        functools.partial(attend_kernel, marks, share),
        grid=(width // LANES,),
        out_shape=jax.ShapeDtypeStruct((total, width), jnp.bfloat16),
        in_specs=[anywhere] * (2 + len(pieces)),
        out_specs=pl.BlockSpec((total, LANES), lambda h: (0, h)),
        scratch_shapes=[
            pltpu.VMEM((length, width), jnp.bfloat16),
            pltpu.VMEM((total, width), jnp.bfloat16),
            pltpu.VMEM((3 * width, width), jnp.bfloat16),
            pltpu.VMEM((2, total, LANES), jnp.bfloat16),
            pltpu.VMEM((2, length, LANES), jnp.bfloat16),
            pltpu.VMEM((2, length, LANES), jnp.bfloat16),
            pltpu.SemaphoreType.DMA((lax.axis_size("dp"),)),
            pltpu.SemaphoreType.DMA((5,)),
        ],
        compiler_params=pltpu.CompilerParams(vmem_limit_bytes=VMEM),
        cost_estimate=pl.CostEstimate(
            flops=16 * total * length * width + 2 * width * width * (total + 2 * length),
            bytes_accessed=2 * width * (3 * width + 3 * total + length),
            transcendentals=total * length * width // HEAD,
        ),
        name="attention",
    )(near, far, *[a for _, _, a in pieces])


def tail_kernel(marks, *refs):
    refs = list(refs)
    context, fed_before, fed_own, fed_after = (refs.pop(0) for _ in range(4))
    weight_refs = [refs.pop(0) for _ in marks]
    gain_conv, gain_final, taps, scale, shift = (refs.pop(0) for _ in range(5))
    out, w_output, w_widen, w_narrow, stream, conv_in, gated, shifted, activated, sems = refs
    rows, width = out.shape
    total = rows + 2 * HALO
    block = 256
    devices, share = w_output.shape[:2]
    targets = [(w_output, 0), (w_widen, share), (w_narrow, 3 * share)]
    own = lax.axis_index("dp")
    for (far, number), ref in zip(marks, weight_refs):
        low = (number or 0) * 2 * share
        high = low + ref.shape[0]
        for index, (target, start) in enumerate(targets):
            first, last = max(low, start), min(high, start + target.shape[1])
            if first < last:
                pltpu.make_async_copy(
                    ref.at[first - low : last - low, :],
                    target.at[own ^ far, first - start : last - start],
                    sems.at[index, own ^ far],
                ).start()

    def arrived(index):
        for owner in range(devices):
            place = targets[index][0].at[owner]
            pltpu.make_async_copy(place, place, sems.at[index, owner]).wait()

    def rows_of(ref, start):
        each = ref.shape[1]
        return ref[start // each : (start + block) // each].reshape(block, width)

    arrived(0)
    for start in range(0, width, block):
        columns = slice(start, start + block)
        mixed = product(context[...], rows_of(w_output, start))
        stream[0:HALO, columns] = fed_before[:, columns] + mixed[0:HALO]
        stream[HALO : HALO + rows, columns] = fed_own[:, columns] + mixed[HALO : HALO + rows]
        stream[HALO + rows :, columns] = fed_after[:, columns] + mixed[HALO + rows :]
    conv_in[...] = kernel_norm(stream[...], gain_conv[...]).astype(jnp.bfloat16)

    arrived(1)
    place = lax.broadcasted_iota(jnp.int32, (total, block), 0)
    here, last = lax.axis_index("seq"), lax.axis_size("seq") - 1
    low = jnp.where(here == 0, HALO, 0)
    high = jnp.where(here == last, HALO + rows, total)
    inside = jnp.logical_and(place >= low, place < high)
    for start in range(0, width, block):
        columns = slice(start, start + block)
        left = product(conv_in[...], rows_of(w_widen, start))
        right = product(conv_in[...], rows_of(w_widen, width + start))
        gate = (left * (0.5 + 0.5 * jnp.tanh(0.5 * right))).astype(jnp.bfloat16)
        gated[:, columns] = jnp.where(inside, gate.astype(jnp.float32), 0.0)

    lead = HALO - KERNEL // 2
    tile = min(128, rows)

    def conv(index, carry):
        columns = pl.ds(pl.multiple_of(index * LANES, LANES), LANES)
        for residue in range(1, 8):
            shifted[residue, 0 : total - 8, :] = gated[residue : residue + total - 8, columns]
        for start in range(0, rows, tile):
            filtered = jnp.zeros((tile, LANES), jnp.float32)
            for tap in range(KERNEL):
                offset = tap + lead
                base = start + offset // 8 * 8
                if offset % 8 == 0:
                    piece = gated[base : base + tile, columns]
                else:
                    piece = shifted[offset % 8, base : base + tile, :]
                filtered = filtered + taps[tap : tap + 1, columns] * piece
            moved = filtered * scale[:, columns] + shift[:, columns]
            activated[start : start + tile, columns] = silu(moved).astype(jnp.bfloat16)
        return carry

    lax.fori_loop(0, width // LANES, conv, 0)

    arrived(2)
    for start in range(0, width, block):
        columns = slice(start, start + block)
        stream[HALO : HALO + rows, columns] += product(activated[...], rows_of(w_narrow, start))
    out[...] = kernel_norm(stream[HALO : HALO + rows, :], gain_final[...]).astype(jnp.bfloat16)


def tail_of(context, fed_before, fed_own, fed_after, pieces, gain_conv, gain_final, taps, scale, shift):
    rows, width = fed_own.shape
    total = rows + 2 * HALO
    devices = lax.axis_size("dp")
    share = width // devices
    marks = [piece[:2] for piece in pieces]
    whole = pl.BlockSpec(memory_space=pltpu.VMEM)
    return pl.pallas_call(
        functools.partial(tail_kernel, marks),
        out_shape=jax.ShapeDtypeStruct((rows, width), jnp.bfloat16),
        in_specs=[whole] * 4
        + [pl.BlockSpec(memory_space=pl.ANY)] * len(pieces)
        + [whole] * 5,
        out_specs=whole,
        scratch_shapes=[
            pltpu.VMEM((devices, share, width), jnp.bfloat16),
            pltpu.VMEM((devices, 2 * share, width), jnp.bfloat16),
            pltpu.VMEM((devices, share, width), jnp.bfloat16),
            pltpu.VMEM((total, width), jnp.float32),
            pltpu.VMEM((total, width), jnp.bfloat16),
            pltpu.VMEM((total, width), jnp.float32),
            pltpu.VMEM((8, total, LANES), jnp.float32),
            pltpu.VMEM((rows, width), jnp.bfloat16),
            pltpu.SemaphoreType.DMA((3, devices)),
        ],
        compiler_params=pltpu.CompilerParams(vmem_limit_bytes=36 << 20),
        cost_estimate=pl.CostEstimate(
            flops=8 * total * width * width + 2 * KERNEL * rows * width,
            bytes_accessed=8 * width * width + 10 * rows * width,
            transcendentals=3 * rows * width,
        ),
        name="tail",
    )(
        context, fed_before, fed_own, fed_after, *[a for _, _, a in pieces],
        gain_conv[None], gain_final[None], taps, scale[None], shift[None],
    )


def body(
    tokens,
    expand_value,
    expand_scale,
    shrink_value,
    shrink_scale,
    project_value,
    project_scale,
    output_value,
    output_scale,
    widen_value,
    widen_scale,
    narrow_value,
    narrow_scale,
    kernel_taps,
    gain_feed,
    gain_attend,
    gain_conv,
    gain_final,
    batch_scale,
    batch_shift,
):
    count = lax.axis_size("seq")
    rows = tokens.shape[1]
    ring = [(i, (i + 1) % count) for i in range(count)]
    before = lax.ppermute(tokens[0], "seq", ring)
    after = lax.ppermute(tokens[0], "seq", [(b, a) for a, b in ring])
    expand_sets, shrink_sets = (
        [one]
        for one in first_stages(
            [own_rows_of(expand_value, expand_scale), own_rows_of(shrink_value, shrink_scale)]
        )
    )
    project_rows = own_rows_of(project_value, project_scale)
    tail_rows = jnp.concatenate(
        [
            own_rows_of(output_value, output_scale),
            own_rows_of(widen_value, widen_scale),
            own_rows_of(narrow_value, narrow_scale),
        ],
        axis=0,
    )

    arrays, project_rows, tail_rows = barrier(flat(expand_sets), project_rows, tail_rows)
    expand_near, expand_late = split_late(later_stages(refilled(expand_sets, arrays)))
    expand_near = crossed(expand_near)

    arrays, expand_near = held_back(flat(shrink_sets), expand_near)
    shrink_near, shrink_late = split_late(later_stages(refilled(shrink_sets, arrays)))
    shrink_near = crossed(shrink_near)

    late, pieces, project_rows, tail_rows, before, after = barrier(
        [t[2] for t in expand_late + shrink_late],
        [t[2] for t in expand_near + shrink_near],
        project_rows,
        tail_rows,
        before,
        after,
    )
    pieces = replaced(expand_near + shrink_near, pieces)
    pieces += crossed(replaced(expand_late + shrink_late, late))
    others = [before]
    while len(others) < count - 2:
        others.append(lax.ppermute(others[-1], "seq", ring))
    others = others[1:]
    project_near = first_sends(project_rows)
    project_own = crossed(project_near[:1])
    tail_own = crossed([(0, None, tail_rows)])
    expand_pieces, shrink_pieces = by_part(pieces)

    attend_near, fed_before, fed_after, after_feed = feed(
        [tokens[0], before, after], [(1, rows - HALO), (2, 0)], True,
        gain_feed, gain_attend, expand_pieces, shrink_pieces,
    )
    attend_near, arrays, tail_rows = barrier(
        attend_near, [t[2] for t in project_near], tail_rows
    )
    project_near = replaced(project_near, arrays)
    project_late = relays(project_near)
    project_near = project_own + crossed(project_near[1:])
    tail_far = [
        (far, None, send(tail_rows, far)) for far in range(2, lax.axis_size("dp"), 2)
    ]
    (attend_far,) = feed(
        others, [], False, gain_feed, gain_attend, expand_pieces, shrink_pieces
    )
    attend_far, late = barrier(attend_far, [t[2] for t in project_late])
    project_pieces = project_near + crossed(replaced(project_late, late))
    context = attention(rows, attend_near, attend_far, project_pieces)
    context, arrays = barrier(context, [t[2] for t in tail_far])
    tail_pieces = tail_own + crossed(replaced(tail_far, arrays))
    return tail_of(
        context, fed_before, after_feed, fed_after, tail_pieces,
        gain_conv, gain_final, kernel_taps, batch_scale, batch_shift,
    )[None]


def solution(mesh):
    weights = (P(None, "dp"),) * 12
    return jax.shard_map(
        body,
        mesh=mesh,
        in_specs=(P("dp", "seq", None),) + weights + (P(),) * 7,
        out_specs=P("dp", "seq", None),
        check_vma=False,
    )
```

```python
import functools

import jax
import jax.numpy as jnp
from jax import lax
from jax.experimental import pallas as pl
from jax.experimental.layout import Layout, with_layout_constraint
from jax.experimental.pallas import tpu as pltpu
from jax.sharding import PartitionSpec as P

HEAD = 64
KERNEL = 31
LANES = 128
HALO = 16
VMEM = 60 << 20
NT = (((1,), (1,)), ((), ()))


def dequant(value_grid, scale_grid):
    stretched = jnp.repeat(scale_grid.astype(jnp.float32), 128, axis=0)
    return (value_grid.astype(jnp.float32) * stretched).astype(jnp.bfloat16)


def own_rows_of(value_grid, scale_grid):
    return jnp.transpose(dequant(value_grid, scale_grid))


def gathered(rows):
    return lax.all_gather(rows, "dp", axis=0, tiled=True)


def product(left, right):
    return lax.dot_general(left, right, NT, preferred_element_type=jnp.float32)


def layer_norm(values, gain_row):
    average = jnp.mean(values, axis=-1, keepdims=True)
    centred = values - average
    energy = jnp.mean(centred * centred, axis=-1, keepdims=True)
    return centred * lax.rsqrt(energy + 1e-05) * gain_row


def partners(size, bit):
    return [(i, i ^ bit) for i in range(size)]


def send(array, bit):
    return lax.ppermute(array, "dp", partners(lax.axis_size("dp"), bit))


def far_bits():
    return [1 << b for b in range(1, lax.axis_size("dp").bit_length() - 1)]


def stage(held, bit):
    return held + [(far ^ bit, number, send(a, bit)) for far, number, a in held]


def first_stages(parts):
    bits = far_bits()
    return [
        ([(0, number, part)], [(bit, number, send(part, bit)) for bit in bits])
        for number, part in enumerate(parts)
    ]


def later_stages(sets):
    bits = far_bits()
    result = []
    for own, first in sets:
        number = own[0][1]
        order = bits if number % 2 == 0 else bits[::-1]
        by_bit = dict(zip(bits, first))
        held = list(own)
        for bit in order:
            held += [by_bit[bit]] + [(far ^ bit, n, send(a, bit)) for far, n, a in held[1:]]
        result += held
    return result


def first_sends(array):
    return [(0, None, array)] + [(bit, None, send(array, bit)) for bit in far_bits()]


def relays(first):
    bits = far_bits()
    arrived = {far: array for far, _, array in first}
    result = []
    for number, order in ((0, bits), (1, bits[::-1])):
        half = arrived[0].shape[0] // 2
        cut = {bit: arrived[bit][number * half : (number + 1) * half] for bit in bits}
        held = [(order[0], cut[order[0]])]
        for bit in order[1:]:
            sent = [(far ^ bit, send(a, bit)) for far, a in held]
            held += [(bit, cut[bit])] + sent
            result += [(far, number, a) for far, a in sent]
    return result


def flat(sets):
    return [a for own, first in sets for _, _, a in own + first]


def split_late(held):
    near = [0, *far_bits()]
    return [t for t in held if t[0] in near], [t for t in held if t[0] not in near]


def by_part(pieces):
    return [
        sorted([(far, a) for far, n, a in pieces if n == part], key=lambda t: t[0])
        for part in (0, 1)
    ]


def replaced(held, arrays):
    return [(far, number, a) for (far, number, _), a in zip(held, arrays)]


def held_back(arrays, held):
    arrays, others = barrier(arrays, [a for _, _, a in held])
    return arrays, replaced(held, others)


def crossed(held):
    return stage(held, 1)


def refilled(sets, arrays):
    arrays = list(arrays)
    return [
        tuple([(far, n, arrays.pop(0)) for far, n, _ in group] for group in pair) for pair in sets
    ]


def barrier(*trees):
    return lax.optimization_barrier(trees)


def copies(fars, refs, target, sems):
    own = lax.axis_index("dp")
    made = []
    for far, ref in zip(fars, refs):
        owner = own ^ far
        start = pl.multiple_of(owner * ref.shape[0], 16)
        rows = target.at[pl.ds(start, ref.shape[0]), :]
        made.append(pltpu.make_async_copy(ref, rows, sems.at[owner]))
    return made


def wait_rows(target, sems, share, owners):
    for owner in owners:
        rows = target.at[owner * share : (owner + 1) * share, :]
        pltpu.make_async_copy(rows, rows, sems.at[owner]).wait()


def half_copies(marks, refs, target, sems, share):
    own = lax.axis_index("dp")
    made = []
    for (far, number), ref in zip(marks, refs):
        owner = own ^ far
        start = pl.multiple_of(owner * share + (number or 0) * (share // 2), 16)
        rows = target.at[pl.ds(start, ref.shape[0]), :]
        made.append(pltpu.make_async_copy(ref, rows, sems.at[owner]))
    return made


def kernel_norm(values, gain_row):
    scale = 1.0 / values.shape[1]
    average = jnp.sum(values, axis=1, keepdims=True) * scale
    centred = values - average
    energy = jnp.sum(centred * centred, axis=1, keepdims=True) * scale
    return centred * lax.rsqrt(energy + 1e-05) * gain_row


def silu(v):
    half = 0.5 * v
    return half + half * jnp.tanh(half)


def feed_kernel(chunks, fars, edges, keep, *refs):
    refs = list(refs)
    tokens = [refs.pop(0) for _ in range(chunks)]
    gain_feed, gain_attend = refs.pop(0), refs.pop(0)
    expand_refs = [refs.pop(0) for _ in fars]
    shrink_refs = [refs.pop(0) for _ in fars]
    attend_in = refs.pop(0)
    fed_edges = [refs.pop(0) for _ in edges]
    fed = refs.pop(0) if keep else None
    held, expand_all, shrink_all, feed_in, hidden, total, token_sems, expand_sems, shrink_sems = refs
    step = pl.program_id(0)
    units, width = expand_all.shape
    block = 256
    token_copies = [
        pltpu.make_async_copy(t, held.at[i], token_sems.at[i]) for i, t in enumerate(tokens)
    ]

    @pl.when(step == 0)
    def _():
        token_copies[0].start()
        for copy in copies(fars, expand_refs, expand_all, expand_sems):
            copy.start()

    for i in range(chunks):
        @pl.when(step == i)
        def _(i=i):
            token_copies[i].wait()

    own = held[step].astype(jnp.float32)
    feed_in[...] = kernel_norm(own, gain_feed[...]).astype(jnp.bfloat16)

    @pl.when(step == 0)
    def _():
        wait_rows(expand_all, expand_sems, units // len(fars), range(len(fars)))
        for copy in copies(fars, shrink_refs, shrink_all, shrink_sems) + token_copies[1:]:
            copy.start()

    for n in range(units // block):
        piece = slice(n * block, (n + 1) * block)
        hidden[:, piece] = silu(product(feed_in[...], expand_all[piece, :])).astype(jnp.bfloat16)

    @pl.when(step == 0)
    def _():
        wait_rows(shrink_all, shrink_sems, width // len(fars), range(len(fars)))

    for n in range(width // block):
        piece = slice(n * block, (n + 1) * block)
        total[:, piece] = held[step, :, piece].astype(jnp.float32) + 0.5 * product(
            hidden[...], shrink_all[piece, :]
        )
    attend_in[...] = kernel_norm(total[...], gain_attend[...]).astype(jnp.bfloat16)
    if fed is not None:

        @pl.when(step == 0)
        def _():
            fed[...] = total[...]

    for (place, start), fed_edge in zip(edges, fed_edges):

        @pl.when(step == place)
        def _(start=start, fed_edge=fed_edge):
            fed_edge[...] = total[start : start + HALO, :]


def feed(chunks, edges, keep, gain_feed, gain_attend, expand_pieces, shrink_pieces):
    rows, width = chunks[0].shape
    count, devices = len(chunks), len(expand_pieces)
    units = devices * expand_pieces[0][1].shape[0]
    fars = [far for far, _ in expand_pieces]
    anywhere = pl.BlockSpec(memory_space=pltpu.HBM)
    row = pl.BlockSpec((1, width), lambda i: (0, 0))
    return pl.pallas_call(
        functools.partial(feed_kernel, count, fars, edges, keep),
        grid=(count,),
        out_shape=[
            jax.ShapeDtypeStruct((count * rows, width), jnp.bfloat16),
        ]
        + [jax.ShapeDtypeStruct((HALO, width), jnp.float32)] * len(edges)
        + [jax.ShapeDtypeStruct((rows, width), jnp.float32)] * keep,
        in_specs=[anywhere] * count + [row, row] + [anywhere] * (2 * devices),
        out_specs=[
            pl.BlockSpec((rows, width), lambda i: (i, 0)),
        ]
        + [pl.BlockSpec((HALO, width), lambda i: (0, 0))] * len(edges)
        + [pl.BlockSpec((rows, width), lambda i: (0, 0))] * keep,
        scratch_shapes=[
            pltpu.VMEM((count, rows, width), jnp.bfloat16),
            pltpu.VMEM((units, width), jnp.bfloat16),
            pltpu.VMEM((width, units), jnp.bfloat16),
            pltpu.VMEM((rows, width), jnp.bfloat16),
            pltpu.VMEM((rows, units), jnp.bfloat16),
            pltpu.VMEM((rows, width), jnp.float32),
            pltpu.SemaphoreType.DMA((count,)),
            pltpu.SemaphoreType.DMA((devices,)),
            pltpu.SemaphoreType.DMA((devices,)),
        ],
        compiler_params=pltpu.CompilerParams(vmem_limit_bytes=VMEM),
        cost_estimate=pl.CostEstimate(
            flops=4 * count * rows * width * units,
            bytes_accessed=4 * units * width + 4 * count * rows * width,
            transcendentals=count * rows * units,
        ),
        name="feed",
    )(
        *chunks, gain_feed[None], gain_attend[None],
        *[a for _, a in expand_pieces], *[a for _, a in shrink_pieces],
    )


def attend_kernel(marks, share, *refs):
    near, far = refs[:2]
    weight_refs = refs[2 : 2 + len(marks)]
    out_ref, inputs, query_rows, weights, queries, keys, values, sems, row_sems = refs[
        2 + len(marks) :
    ]
    step, steps = pl.program_id(0), pl.num_programs(0)
    length, width = inputs.shape
    rows = query_rows.shape[0] - 2 * HALO
    pairs = width // LANES
    made = half_copies(marks, weight_refs, weights, sems, share)
    soon = sorted({(part * width + pair * LANES) // share for part in range(3) for pair in (0, 1)})
    row_copies = [
        pltpu.make_async_copy(source, target, row_sems.at[index])
        for index, (source, target) in enumerate(
            (
                (near.at[0:rows, :], query_rows.at[HALO : HALO + rows, :]),
                (near.at[2 * rows - HALO : 2 * rows, :], query_rows.at[0:HALO, :]),
                (near.at[2 * rows : 2 * rows + HALO, :], query_rows.at[HALO + rows :, :]),
                (near, inputs.at[0 : near.shape[0], :]),
                (far, inputs.at[near.shape[0] :, :]),
            )
        )
    ]
    rest = [owner for owner in range(3 * width // share) if owner not in soon]
    here = lax.axis_index("dp")

    def start_owned(owners):
        for (far, _), copy in zip(marks, made):
            owner = here ^ far
            wanted = functools.reduce(jnp.logical_or, [owner == o for o in owners])

            @pl.when(wanted)
            def _(copy=copy):
                copy.start()

    def project_queries(pair, slot):
        picked = weights[pl.ds(pl.multiple_of(pair * LANES, LANES), LANES), :]
        scaled = product(query_rows[...], picked).astype(jnp.bfloat16) * HEAD ** (-0.5)
        queries[slot] = scaled.astype(jnp.bfloat16)

    def project_pair(pair, slot, start, stop):
        first = pl.ds(pl.multiple_of(width + pair * LANES, LANES), LANES)
        second = pl.ds(pl.multiple_of(2 * width + pair * LANES, LANES), LANES)
        both = jnp.concatenate([weights[first, :], weights[second, :]], axis=0)
        made_rows = product(inputs[start:stop, :], both).astype(jnp.bfloat16)
        keys[slot, start:stop, :] = made_rows[:, :LANES]
        values[slot, start:stop, :] = made_rows[:, LANES:]

    @pl.when(step == 0)
    def _():
        for copy in row_copies:
            copy.start()
        start_owned(soon)
        for copy in row_copies:
            copy.wait()
        wait_rows(weights, sems, share, soon)
        start_owned(rest)
        project_queries(0, 0)
        for start in range(0, length, rows):
            project_pair(0, 0, start, start + rows)

    @pl.when(step == 1)
    def _():
        wait_rows(weights, sems, share, rest)

    slot = lax.rem(step, 2)
    heads = LANES // HEAD
    tile = query_rows.shape[0] // 2
    lane = lax.broadcasted_iota(jnp.int32, (tile, LANES), 1) // HEAD
    tiles = [(start, head) for start in (0, tile) for head in range(heads)]
    blocks = [slice(start, start + rows) for start in range(0, length, rows)]

    def scores_of(start, head):
        picked = jnp.where(lane == head, queries[slot, start : start + tile, :], jnp.bfloat16(0))
        return [product(picked, keys[slot, block, :]) for block in blocks]

    def context_of(scores):
        top = functools.reduce(jnp.maximum, [jnp.max(s, axis=1, keepdims=True) for s in scores])
        raised = [jnp.exp(s - top) for s in scores]
        totals = sum(jnp.sum(r, axis=1, keepdims=True) for r in raised)
        mixed = sum(
            jnp.dot(
                r.astype(jnp.bfloat16),
                values[slot, block, :],
                preferred_element_type=jnp.float32,
            )
            for r, block in zip(raised, blocks)
        )
        return mixed / totals

    def attend(project):
        pending = scores_of(*tiles[0])
        merged = None
        for index, (start, head) in enumerate(tiles):
            scores = pending
            if index + 1 < len(tiles):
                pending = scores_of(*tiles[index + 1])
            if project:
                if index == 0:
                    project_queries(step + 1, 1 - slot)
                for block in blocks[index :: len(tiles)]:
                    project_pair(step + 1, 1 - slot, block.start, block.stop)
            mixed = context_of(scores)
            merged = mixed if head == 0 else jnp.where(lane == head, mixed, merged)
            if head == heads - 1:
                out_ref[start : start + tile, :] = merged.astype(jnp.bfloat16)

    @pl.when(step < steps - 1)
    def _():
        attend(True)

    @pl.when(step == steps - 1)
    def _():
        attend(False)


def attention(rows, near, far, pieces):
    width = far.shape[1]
    total = rows + 2 * HALO
    length = near.shape[0] + far.shape[0]
    anywhere = pl.BlockSpec(memory_space=pltpu.HBM)
    marks = [piece[:2] for piece in pieces]
    share = 3 * width // lax.axis_size("dp")
    return pl.pallas_call(
        functools.partial(attend_kernel, marks, share),
        grid=(width // LANES,),
        out_shape=jax.ShapeDtypeStruct((total, width), jnp.bfloat16),
        in_specs=[anywhere] * (2 + len(pieces)),
        out_specs=pl.BlockSpec((total, LANES), lambda h: (0, h)),
        scratch_shapes=[
            pltpu.VMEM((length, width), jnp.bfloat16),
            pltpu.VMEM((total, width), jnp.bfloat16),
            pltpu.VMEM((3 * width, width), jnp.bfloat16),
            pltpu.VMEM((2, total, LANES), jnp.bfloat16),
            pltpu.VMEM((2, length, LANES), jnp.bfloat16),
            pltpu.VMEM((2, length, LANES), jnp.bfloat16),
            pltpu.SemaphoreType.DMA((lax.axis_size("dp"),)),
            pltpu.SemaphoreType.DMA((5,)),
        ],
        compiler_params=pltpu.CompilerParams(vmem_limit_bytes=VMEM),
        cost_estimate=pl.CostEstimate(
            flops=16 * total * length * width + 2 * width * width * (total + 2 * length),
            bytes_accessed=2 * width * (3 * width + 3 * total + length),
            transcendentals=total * length * width // HEAD,
        ),
        name="attention",
    )(near, far, *[a for _, _, a in pieces])


def tail_kernel(marks, *refs):
    refs = list(refs)
    context, fed_before, fed_own, fed_after = (refs.pop(0) for _ in range(4))
    weight_refs = [refs.pop(0) for _ in marks]
    gain_conv, gain_final, taps, scale, shift = (refs.pop(0) for _ in range(5))
    out, w_output, w_widen, w_narrow, stream, conv_in, gated, shifted, activated, sems = refs
    rows, width = out.shape
    total = rows + 2 * HALO
    block = 256
    devices, share = w_output.shape[:2]
    targets = [(w_output, 0), (w_widen, share), (w_narrow, 3 * share)]
    own = lax.axis_index("dp")
    for (far, number), ref in zip(marks, weight_refs):
        low = (number or 0) * 2 * share
        high = low + ref.shape[0]
        for index, (target, start) in enumerate(targets):
            first, last = max(low, start), min(high, start + target.shape[1])
            if first < last:
                pltpu.make_async_copy(
                    ref.at[first - low : last - low, :],
                    target.at[own ^ far, first - start : last - start],
                    sems.at[index, own ^ far],
                ).start()

    def arrived(index):
        for owner in range(devices):
            place = targets[index][0].at[owner]
            pltpu.make_async_copy(place, place, sems.at[index, owner]).wait()

    def rows_of(ref, start):
        each = ref.shape[1]
        return ref[start // each : (start + block) // each].reshape(block, width)

    arrived(0)
    for start in range(0, width, block):
        columns = slice(start, start + block)
        mixed = product(context[...], rows_of(w_output, start))
        stream[0:HALO, columns] = fed_before[:, columns] + mixed[0:HALO]
        stream[HALO : HALO + rows, columns] = fed_own[:, columns] + mixed[HALO : HALO + rows]
        stream[HALO + rows :, columns] = fed_after[:, columns] + mixed[HALO + rows :]
    conv_in[...] = kernel_norm(stream[...], gain_conv[...]).astype(jnp.bfloat16)

    arrived(1)
    place = lax.broadcasted_iota(jnp.int32, (total, block), 0)
    here, last = lax.axis_index("seq"), lax.axis_size("seq") - 1
    low = jnp.where(here == 0, HALO, 0)
    high = jnp.where(here == last, HALO + rows, total)
    inside = jnp.logical_and(place >= low, place < high)
    for start in range(0, width, block):
        columns = slice(start, start + block)
        left = product(conv_in[...], rows_of(w_widen, start))
        right = product(conv_in[...], rows_of(w_widen, width + start))
        gate = (left * (0.5 + 0.5 * jnp.tanh(0.5 * right))).astype(jnp.bfloat16)
        gated[:, columns] = jnp.where(inside, gate.astype(jnp.float32), 0.0)

    lead = HALO - KERNEL // 2
    tile = min(128, rows)

    def conv(index, carry):
        columns = pl.ds(pl.multiple_of(index * LANES, LANES), LANES)
        for residue in range(1, 8):
            shifted[residue, 0 : total - 8, :] = gated[residue : residue + total - 8, columns]
        for start in range(0, rows, tile):
            filtered = jnp.zeros((tile, LANES), jnp.float32)
            for tap in range(KERNEL):
                offset = tap + lead
                base = start + offset // 8 * 8
                if offset % 8 == 0:
                    piece = gated[base : base + tile, columns]
                else:
                    piece = shifted[offset % 8, base : base + tile, :]
                filtered = filtered + taps[tap : tap + 1, columns] * piece
            moved = filtered * scale[:, columns] + shift[:, columns]
            activated[start : start + tile, columns] = silu(moved).astype(jnp.bfloat16)
        return carry

    lax.fori_loop(0, width // LANES, conv, 0)

    arrived(2)
    for start in range(0, width, block):
        columns = slice(start, start + block)
        stream[HALO : HALO + rows, columns] += product(activated[...], rows_of(w_narrow, start))
    out[...] = kernel_norm(stream[HALO : HALO + rows, :], gain_final[...]).astype(jnp.bfloat16)


def tail_of(context, fed_before, fed_own, fed_after, pieces, gain_conv, gain_final, taps, scale, shift):
    rows, width = fed_own.shape
    total = rows + 2 * HALO
    devices = lax.axis_size("dp")
    share = width // devices
    marks = [piece[:2] for piece in pieces]
    whole = pl.BlockSpec(memory_space=pltpu.VMEM)
    return pl.pallas_call(
        functools.partial(tail_kernel, marks),
        out_shape=jax.ShapeDtypeStruct((rows, width), jnp.bfloat16),
        in_specs=[whole] * 4
        + [pl.BlockSpec(memory_space=pl.ANY)] * len(pieces)
        + [whole] * 5,
        out_specs=whole,
        scratch_shapes=[
            pltpu.VMEM((devices, share, width), jnp.bfloat16),
            pltpu.VMEM((devices, 2 * share, width), jnp.bfloat16),
            pltpu.VMEM((devices, share, width), jnp.bfloat16),
            pltpu.VMEM((total, width), jnp.float32),
            pltpu.VMEM((total, width), jnp.bfloat16),
            pltpu.VMEM((total, width), jnp.float32),
            pltpu.VMEM((8, total, LANES), jnp.float32),
            pltpu.VMEM((rows, width), jnp.bfloat16),
            pltpu.SemaphoreType.DMA((3, devices)),
        ],
        compiler_params=pltpu.CompilerParams(vmem_limit_bytes=36 << 20),
        cost_estimate=pl.CostEstimate(
            flops=8 * total * width * width + 2 * KERNEL * rows * width,
            bytes_accessed=8 * width * width + 10 * rows * width,
            transcendentals=3 * rows * width,
        ),
        name="tail",
    )(
        context, fed_before, fed_own, fed_after, *[a for _, _, a in pieces],
        gain_conv[None], gain_final[None], taps, scale[None], shift[None],
    )


def body(
    tokens,
    expand_value,
    expand_scale,
    shrink_value,
    shrink_scale,
    project_value,
    project_scale,
    output_value,
    output_scale,
    widen_value,
    widen_scale,
    narrow_value,
    narrow_scale,
    kernel_taps,
    gain_feed,
    gain_attend,
    gain_conv,
    gain_final,
    batch_scale,
    batch_shift,
):
    count = lax.axis_size("seq")
    rows = tokens.shape[1]
    ring = [(i, (i + 1) % count) for i in range(count)]
    before = lax.ppermute(tokens[0], "seq", ring)
    after = lax.ppermute(tokens[0], "seq", [(b, a) for a, b in ring])
    expand_sets, shrink_sets = (
        [one]
        for one in first_stages(
            [own_rows_of(expand_value, expand_scale), own_rows_of(shrink_value, shrink_scale)]
        )
    )
    project_rows = own_rows_of(project_value, project_scale)
    tail_rows = jnp.concatenate(
        [
            own_rows_of(output_value, output_scale),
            own_rows_of(widen_value, widen_scale),
            own_rows_of(narrow_value, narrow_scale),
        ],
        axis=0,
    )

    arrays, project_rows, tail_rows = barrier(flat(expand_sets), project_rows, tail_rows)
    expand_near, expand_late = split_late(later_stages(refilled(expand_sets, arrays)))
    expand_near = crossed(expand_near)

    arrays, expand_near = held_back(flat(shrink_sets), expand_near)
    shrink_near, shrink_late = split_late(later_stages(refilled(shrink_sets, arrays)))
    shrink_near = crossed(shrink_near)

    late, pieces, project_rows, tail_rows, before, after = barrier(
        [t[2] for t in expand_late + shrink_late],
        [t[2] for t in expand_near + shrink_near],
        project_rows,
        tail_rows,
        before,
        after,
    )
    pieces = replaced(expand_near + shrink_near, pieces)
    pieces += crossed(replaced(expand_late + shrink_late, late))
    others = [before]
    while len(others) < count - 2:
        others.append(lax.ppermute(others[-1], "seq", ring))
    others = others[1:]
    project_near = first_sends(project_rows)
    project_own = crossed(project_near[:1])
    tail_own = crossed([(0, None, tail_rows)])
    expand_pieces, shrink_pieces = by_part(pieces)

    attend_near, fed_before, fed_after, after_feed = feed(
        [tokens[0], before, after], [(1, rows - HALO), (2, 0)], True,
        gain_feed, gain_attend, expand_pieces, shrink_pieces,
    )
    attend_near, arrays, tail_rows = barrier(
        attend_near, [t[2] for t in project_near], tail_rows
    )
    project_near = replaced(project_near, arrays)
    project_late = relays(project_near)
    project_near = project_own + crossed(project_near[1:])
    tail_far = [
        (far, None, send(tail_rows, far)) for far in range(2, lax.axis_size("dp"), 2)
    ]
    (attend_far,) = feed(
        others, [], False, gain_feed, gain_attend, expand_pieces, shrink_pieces
    )
    attend_far, late = barrier(attend_far, [t[2] for t in project_late])
    project_pieces = project_near + crossed(replaced(project_late, late))
    context = attention(rows, attend_near, attend_far, project_pieces)
    context, arrays = barrier(context, [t[2] for t in tail_far])
    tail_pieces = tail_own + crossed(replaced(tail_far, arrays))
    return tail_of(
        context, fed_before, after_feed, fed_after, tail_pieces,
        gain_conv, gain_final, kernel_taps, batch_scale, batch_shift,
    )[None]


def solution(mesh):
    weights = (P(None, "dp"),) * 12
    return jax.shard_map(
        body,
        mesh=mesh,
        in_specs=(P("dp", "seq", None),) + weights + (P(),) * 7,
        out_specs=P("dp", "seq", None),
        check_vma=False,
    )
```
